32 devices in a mesh: groups: 2 (over y), dp: 4 (over z), section: 4 (over x, core).
Axes of the slice: x: 2, y: 2, z: 4, core: 2. Of those that a mesh axis runs over, the one named last changes fastest.
Arguments:
- top_pair: bfloat16 [3072, 3072], P(('groups', 'dp')), parts along dimension 0, may hold values from -48 to 48
- kept: int32 [8], P('groups'), parts along dimension 0, may hold values from 128 to 384, as said below
- teacher: int32 [8], P('groups'), parts along dimension 0, may hold values from -1024 to 1023
- down_proj: bfloat16 [4, 2, 1536, 256], P('section', None, 'dp'), may hold values from -0.15625 to 0.15625
- up_proj: bfloat16 [4, 2, 256, 1536], P('section', None, 'dp'), may hold values from -0.375 to 0.375
- gains: bfloat16 [4, 2, 1536], P('section'), may hold values from 0.099609375 to 1.8984375
- head_proj: bfloat16 [3072, 128], P('dp'), may hold values from -0.109375 to 0.109375
- head_gain: bfloat16 [3072], replicated, may hold values from 0.099609375 to 1.8984375
- head_out: bfloat16 [128], replicated, may hold values from -0.5 to 0.5
Outputs:
- pair_grads: bfloat16 [4, 3072, 3072], P('section', ('groups', 'dp')), parts along dimension 1
- down_grad: float32 [8, 2, 1536, 256], P(('groups', 'section'), None, 'dp'), parts along dimension 0
- up_grad: float32 [8, 2, 256, 1536], P(('groups', 'section'), None, 'dp'), parts along dimension 0
- gain_grad: float32 [8, 2, 1536], P(('groups', 'section'), None, 'dp'), parts along dimension 0
The draws below stay inside these ranges and needn't reach their ends.
There are 2 independent parts, one for each index of `groups`. The reference program is written for one: setup_inputs(seed, part) draws one part's arguments, and reference() takes and returns one part's arrays. A program takes and returns all parts, laid end to end along the dimension named above; an argument that names none is the same for every part. Nothing has to cross between parts.
Inputs may be any that keep to these rules, and one draw needn't show every extreme that they name: `kept`: in each aligned group of four passages (4i to 4i + 3) exactly one keeps 3 * 128 tokens and the other three keep 128.
All inputs are finite; a program needn't handle non-finite values.
Results may differ from the reference program's by a relative error of at most 0.03.
Values may be sent and summed in bfloat16 or wider, within the bound.
No kernel may reach another device: no remote copies, remote signals or barrier semaphores. Data moves between devices by JAX's collectives and lax.ppermute only.
A program may use at most 128 MiB of HBM per device.

```python
import jax
import jax.numpy as jnp
from jax import lax

D = 3072
H = 1536
RANK = 256
HEAD = 128
UNIT = 128
SLOTS = 384
PASSAGES = 4
LAYERS = 4


def draw_top_pair(key, part):
    keys = jax.random.split(key, 3)
    count = PASSAGES * SLOTS
    columns = jnp.exp(jax.random.uniform(keys[1], (1, D), jnp.float32, jnp.log(0.3), jnp.log(3.0)))
    row_scale = jnp.exp(jax.random.uniform(keys[0], (count, 1), jnp.float32, jnp.log(0.3), jnp.log(3.0)))
    base = jnp.clip(jax.random.normal(keys[2], (count, D), jnp.float32), -4.0, 4.0)
    return (base * row_scale * columns).astype(jnp.bfloat16)


def draw_kept(key, part):
    groups = PASSAGES // 4
    keys = jax.random.split(key, 2)
    heavy = jax.random.randint(keys[0], (groups, 1), 0, 4)
    rotate = jax.random.randint(keys[1], (), 0, 2)
    first = (jnp.asarray(part, jnp.int32) + 2 * rotate) % 4
    heavy = heavy.at[0, 0].set(first.astype(heavy.dtype))
    places = jnp.arange(4, dtype=jnp.int32)[None, :]
    counts = UNIT + 2 * UNIT * (places == heavy).astype(jnp.int32)
    return counts.reshape(PASSAGES).astype(jnp.int32)


def plant(result, stream_key, least, high):
    longest = result.shape.index(max(result.shape))
    spots = []
    for shift in (0, 1):
        where = [jax.random.randint(jax.random.fold_in(stream_key, axis), (), 0, length) for axis, length in enumerate(result.shape)]
        where[longest] = (where[longest] + shift) % result.shape[longest]
        spots.append(tuple(where))
    return result.at[spots[0]].set(least).at[spots[1]].set(high)


def shard_levels(key, shape, cuts, least, top_value):
    def one(position, blocks):
        draws = jax.random.uniform(jax.random.fold_in(jax.random.fold_in(key, 6), position), (blocks,), jnp.float32, least / len(cuts), top_value / len(cuts))
        return jnp.repeat(jnp.exp(draws), shape[position] // blocks).reshape((-1,) + (1,) * (len(shape) - position - 1))

    level = one(*cuts[0])
    for cut in cuts[1:]:
        level = level * one(*cut)
    return level


def normal_values(key, shape, deviation, reach, pieces=(), kind=jnp.bfloat16):
    entries = deviation * jax.random.normal(key, shape, jnp.float32)
    if pieces:
        entries = entries * shard_levels(key, shape, pieces, -0.22, 0.18)
    return jnp.clip(entries, -reach, reach).astype(kind)


def setup_inputs(seed: int = 0, part: int = 0) -> dict:
    key_list = jax.random.split(jax.random.key(seed), 10)
    part_keys = jax.random.split(jax.random.fold_in(key_list[9], part), 10)
    return {
        "top_pair": draw_top_pair(jax.random.fold_in(jax.random.fold_in(key_list[9], part), 71), part),
        "kept": draw_kept(jax.random.fold_in(jax.random.fold_in(key_list[9], part), 71), part),
        "teacher": plant(jax.random.randint(part_keys[2], (PASSAGES,), -1024, 1024), jax.random.fold_in(part_keys[2], 1), -1024, 1023).astype(jnp.int32),
        "down_proj": normal_values(key_list[3], (LAYERS, 2, H, RANK), H ** -0.5, 0.15625, ((0, 4), (2, 4))),
        "up_proj": normal_values(key_list[4], (LAYERS, 2, RANK, H), RANK ** -0.5, 0.375, ((0, 4), (2, 4))),
        "gains": jnp.clip(1.0 + 0.18 * jax.random.normal(key_list[5], (LAYERS, 2, H), jnp.float32), 0.099609375, 1.8984375).astype(jnp.bfloat16),
        "head_proj": normal_values(key_list[6], (D, HEAD), D ** -0.5, 0.109375, ((0, 4),)),
        "head_gain": jnp.clip(1.0 + 0.18 * jax.random.normal(key_list[7], (D,), jnp.float32), 0.099609375, 1.8984375).astype(jnp.bfloat16),
        "head_out": normal_values(key_list[8], (HEAD,), HEAD ** -0.5, 0.5),
    }


EPS = 1e-06
LOSS_SCALE = 4096.0
FIXED_POINT = 256.0

def silu_slope(pre):
    sigma = jax.nn.sigmoid(pre)
    return sigma * (1.0 + pre * (1.0 - sigma))

def branch_forward(inputs, gain, down, upper):
    values = inputs.astype(jnp.float32)
    inverse = lax.rsqrt(lax.optimization_barrier(jnp.mean(values * values, axis=-1, keepdims=True)) + EPS)
    normed = values * inverse
    scaled = (normed * gain.astype(jnp.float32)).astype(jnp.bfloat16)
    pre = jnp.einsum('prh,hk->prk', scaled.astype(jnp.float32), down.astype(jnp.float32))
    hidden = jax.nn.silu(pre).astype(jnp.bfloat16)
    output = jnp.einsum('prk,kh->prh', hidden.astype(jnp.float32), upper.astype(jnp.float32))
    return (output, (inverse, normed, scaled, pre, hidden))

def branch_backward(incoming, saved, gain, down, upper):
    inverse, normed, scaled, pre, hidden = saved
    arriving = incoming.astype(jnp.float32)
    grad_upper = jnp.einsum('prk,prh->pkh', hidden.astype(jnp.float32), arriving)
    grad_hidden = jnp.einsum('prh,kh->prk', arriving, upper.astype(jnp.float32))
    grad_pre = (grad_hidden * silu_slope(pre)).astype(jnp.bfloat16)
    grad_down = jnp.einsum('prh,prk->phk', scaled.astype(jnp.float32), grad_pre.astype(jnp.float32))
    grad_normed = jnp.einsum('prk,hk->prh', grad_pre.astype(jnp.float32), down.astype(jnp.float32))
    grad_gain = lax.optimization_barrier(jnp.sum(grad_normed * normed, axis=1))
    weighted = grad_normed * gain.astype(jnp.float32)
    grad_inputs = inverse * (weighted - normed * lax.optimization_barrier(jnp.mean(normed * weighted, axis=-1, keepdims=True)))
    return (grad_inputs, grad_down, grad_upper, grad_gain)

def passage_mean(partial_value):
    rounded = lax.optimization_barrier(partial_value.astype(jnp.bfloat16))
    return lax.optimization_barrier(jnp.mean(rounded.astype(jnp.float32), axis=0))

def reference(top_pair, kept, teacher, down_proj, up_proj, gains, head_proj, head_gain, head_out):
    passages = kept.shape[0]
    slots = top_pair.shape[0] // passages
    width = top_pair.shape[1]
    half = width // 2
    pair = top_pair.reshape(passages, slots, width)
    live = (jnp.arange(slots, dtype=jnp.int32)[None, :] < kept[:, None]).astype(jnp.float32)
    values = pair.astype(jnp.float32)
    inverse = lax.rsqrt(lax.optimization_barrier(jnp.mean(values * values, axis=-1, keepdims=True)) + EPS)
    normed = values * inverse
    scaled = (normed * head_gain.astype(jnp.float32)).astype(jnp.bfloat16)
    logits = jnp.einsum('prd,dk->prk', scaled.astype(jnp.float32), head_proj.astype(jnp.float32))
    token_scores = lax.optimization_barrier(jnp.sum(jax.nn.silu(logits) * head_out.astype(jnp.float32), axis=-1))
    counts = kept.astype(jnp.float32)
    score = lax.optimization_barrier(jnp.sum(token_scores * live, axis=1)) / counts
    target = teacher.astype(jnp.float32) / FIXED_POINT
    coef = 2.0 * LOSS_SCALE * (score - target) / counts
    grad_scores = coef[:, None] * live
    grad_logits = (grad_scores[..., None] * head_out.astype(jnp.float32) * silu_slope(logits)).astype(jnp.bfloat16)
    grad_normed = jnp.einsum('prk,dk->prd', grad_logits.astype(jnp.float32), head_proj.astype(jnp.float32))
    weighted = grad_normed * head_gain.astype(jnp.float32)
    grad_pair = (inverse * (weighted - normed * lax.optimization_barrier(jnp.mean(normed * weighted, axis=-1, keepdims=True)))).astype(jnp.bfloat16)
    upper_pair = pair
    pair_list = [None] * LAYERS
    down_list = [None] * LAYERS
    upper_list = [None] * LAYERS
    gain_list = [None] * LAYERS
    for layer in range(LAYERS - 1, -1, -1):
        first = upper_pair[..., :half]
        second = upper_pair[..., half:]
        grad_first = grad_pair[..., :half]
        grad_second = grad_pair[..., half:]
        out_second, saved_second = branch_forward(first, gains[layer, 1], down_proj[layer, 1], up_proj[layer, 1])
        lower_second = (second.astype(jnp.float32) - out_second).astype(jnp.bfloat16)
        out_first, saved_first = branch_forward(lower_second, gains[layer, 0], down_proj[layer, 0], up_proj[layer, 0])
        lower_first = (first.astype(jnp.float32) - out_first).astype(jnp.bfloat16)
        back_second = branch_backward(grad_second, saved_second, gains[layer, 1], down_proj[layer, 1], up_proj[layer, 1])
        through_first = (grad_first.astype(jnp.float32) + back_second[0]).astype(jnp.bfloat16)
        back_first = branch_backward(through_first, saved_first, gains[layer, 0], down_proj[layer, 0], up_proj[layer, 0])
        through_second = (grad_second.astype(jnp.float32) + back_first[0]).astype(jnp.bfloat16)
        grad_pair = jnp.concatenate([through_first, through_second], axis=-1)
        upper_pair = jnp.concatenate([lower_first, lower_second], axis=-1)
        pair_list[layer] = grad_pair.reshape(passages * slots, width)
        down_list[layer] = jnp.stack([passage_mean(back_first[1]), passage_mean(back_second[1])])
        upper_list[layer] = jnp.stack([passage_mean(back_first[2]), passage_mean(back_second[2])])
        gain_list[layer] = jnp.stack([passage_mean(back_first[3]), passage_mean(back_second[3])])
    return (jnp.stack(pair_list), jnp.stack(down_list), jnp.stack(upper_list), jnp.stack(gain_list))
```

```python
import functools

import jax
import jax.numpy as jnp
from jax import lax
from jax.experimental import pallas as pl
from jax.experimental.pallas import tpu as pltpu
from jax.sharding import PartitionSpec as P


EPS = 1e-06
LOSS_SCALE = 4096.0
FIXED_POINT = 256.0
QUAD = 4
LONG = 3
F32 = jnp.float32
BF16 = jnp.bfloat16
ANY = pl.BlockSpec(memory_space=pl.ANY)


def dot(left, right):
    return jnp.dot(left, right, preferred_element_type=F32)


def dot_nt(left, right):
    return lax.dot_general(left, right, (((1,), (1,)), ((), ())), preferred_element_type=F32)


def dot_tn(left, right):
    return lax.dot_general(left, right, (((0,), (0,)), ((), ())), preferred_element_type=F32)


def norm_parts(rows):
    values = rows.astype(F32)
    inverse = lax.rsqrt(jnp.mean(values * values, axis=-1, keepdims=True) + EPS)
    return values * inverse, inverse


def head_logits(normed, gain_ref, scaled_ref, meta_ref, pieces):
    scaled_ref[...] = (normed * gain_ref[...].astype(F32)).astype(BF16)
    part = pieces[0].shape[0]
    total = None
    for k, piece in enumerate(pieces):
        start = pl.multiple_of(meta_ref[0, 8 + k] * part, part)
        term = dot(scaled_ref[:, pl.ds(start, part)], piece[...])
        total = term if total is None else total + term
    return total


def score_kernel(count, unit, meta_ref, kept_ref, teacher_ref, rows_ref, gain_ref, out_ref, *rest):
    pieces, (coef_ref, scaled_ref) = rest[:count], rest[count:]
    step = pl.program_id(0)
    kept = kept_ref[meta_ref[0, 5]]

    @pl.when(step == 0)
    def _():
        coef_ref[...] = jnp.zeros_like(coef_ref)

    @pl.when(jnp.logical_and(meta_ref[0, 4] == 1, step * unit < kept))
    def _():
        normed, _ = norm_parts(rows_ref[...])
        logits = head_logits(normed, gain_ref, scaled_ref, meta_ref, pieces)
        scores = jax.nn.silu(logits) * out_ref[...].astype(F32)
        place = lax.broadcasted_iota(jnp.int32, scores.shape, 0) + step * unit
        scores = jnp.where(place < kept, scores, 0.0)
        coef_ref[...] += jnp.broadcast_to(jnp.sum(scores), coef_ref.shape)

    @pl.when(step == pl.num_programs(0) - 1)
    def _():
        counts = jnp.full(coef_ref.shape, kept, jnp.int32).astype(F32)
        target = jnp.full(coef_ref.shape, teacher_ref[meta_ref[0, 5]], jnp.int32).astype(F32)
        score = coef_ref[...] / counts
        coef_ref[...] = 2.0 * LOSS_SCALE * (score - target / FIXED_POINT) / counts


def score_call(meta, kept, teacher, rows, gain, out, pieces, unit):
    slots, width = rows.shape
    keep = lambda *_: (0, 0)
    return pl.pallas_call(
        functools.partial(score_kernel, len(pieces), unit),
        grid_spec=pltpu.PrefetchScalarGridSpec(
            num_scalar_prefetch=3,
            grid=(slots // unit,),
            in_specs=[
                pl.BlockSpec((unit, width), lambda i, *_: (i, 0)),
                pl.BlockSpec(gain.shape, keep),
                pl.BlockSpec(out.shape, keep),
            ]
            + [pl.BlockSpec(p.shape, keep) for p in pieces],
            out_specs=pl.BlockSpec((8, 128), keep),
            scratch_shapes=[pltpu.VMEM((unit, width), BF16)],
        ),
        out_shape=jax.ShapeDtypeStruct((8, 128), F32),
        name="score",
    )(meta, kept, teacher, rows, gain, out, *pieces)


def head_kernel(count, meta_ref, dealt_ref, rows_ref, far_ref, own_ref, gain_ref, out_ref, *rest):
    pieces, (grad_ref, scaled_ref, normal_ref) = rest[:count], rest[count:]
    step = pl.program_id(0)

    @pl.when(meta_ref[0, 4] == 1)
    def _():
        normed, inverse = norm_parts(jnp.where(step == 0, dealt_ref[...], rows_ref[...]))
        normal_ref[...] = normed
        logits = head_logits(normed, gain_ref, scaled_ref, meta_ref, pieces)
        coef = jnp.where(step == 0, far_ref[0:1, :], own_ref[0:1, :])
        sigma = jax.nn.sigmoid(logits)
        slope = sigma * (1.0 + logits * (1.0 - sigma))
        grad = (coef * out_ref[...].astype(F32) * slope).astype(BF16)
        part = pieces[0].shape[0]
        mean = jnp.zeros_like(inverse)
        spans = []
        for k, piece in enumerate(pieces):
            start = pl.multiple_of(meta_ref[0, 8 + k] * part, part)
            span = pl.ds(start, part)
            weighted = dot_nt(grad, piece[...]) * gain_ref[:, span].astype(F32)
            mean += jnp.sum(normal_ref[:, span] * weighted, axis=-1, keepdims=True)
            spans.append((span, weighted))
        mean = mean / normed.shape[1]
        for span, weighted in spans:
            grad_ref[:, span] = (inverse * (weighted - normal_ref[:, span] * mean)).astype(BF16)


def head_call(meta, dealt, rows, far, own, gain, out, pieces, total):
    block, width = dealt.shape
    keep = lambda *_: (0, 0)
    return pl.pallas_call(
        functools.partial(head_kernel, len(pieces)),
        grid_spec=pltpu.PrefetchScalarGridSpec(
            num_scalar_prefetch=1,
            grid=(total // block,),
            in_specs=[
                pl.BlockSpec((block, width), keep),
                pl.BlockSpec((block, width), lambda i, *_: (jnp.maximum(i - 1, 0), 0)),
                pl.BlockSpec((8, 128), keep),
                pl.BlockSpec((8, 128), keep),
                pl.BlockSpec(gain.shape, keep),
                pl.BlockSpec(out.shape, keep),
            ]
            + [pl.BlockSpec(p.shape, keep) for p in pieces],
            out_specs=pl.BlockSpec((block, width), lambda i, *_: (i, 0)),
            scratch_shapes=[pltpu.VMEM((block, width), BF16), pltpu.VMEM((block, width), F32)],
        ),
        out_shape=jax.ShapeDtypeStruct((total, width), BF16),
        name="head",
    )(meta, dealt, rows, far, own, gain, out, *pieces)


def pack_kernel(deals, meta_ref, down_ref, up_ref, rows_ref, *refs):
    outs, (message_s, deal_s, sem) = refs[: 2 + deals], refs[2 + deals :]
    count, part, rank = outs[0].shape[0] // 2, outs[0].shape[1], outs[0].shape[2]
    copies = []

    def copy(source, goal):
        copies.append(pltpu.make_async_copy(source, goal, sem.at[len(copies)]))
        copies[-1].start()

    for number, field in enumerate((3, 6)):
        index = meta_ref[0, field]
        copy(down_ref.at[index], message_s.at[number, pl.ds(0, count)])
        for c in range(count):
            copy(up_ref.at[index, :, pl.ds(c * rank, rank)], message_s.at[number, count + c])
    for k in range(deals):
        rows = deal_s.shape[1]
        start = pl.multiple_of(meta_ref[0, 20 + k], rows)
        copy(rows_ref.at[pl.ds(start, rows)], deal_s.at[k])
    each = 1 + count
    for number in range(2):
        for one in copies[number * each : (number + 1) * each]:
            one.wait()
        copy(message_s.at[number], outs[number])
    for k in range(deals):
        copies[2 * each + k].wait()
        copy(deal_s.at[k], outs[2 + k])
    for one in copies[2 * each + deals :]:
        one.wait()


def pack_call(meta, down, up, rows, deals, chunk):
    part, half = up.shape[1:]
    rank = down.shape[2]
    count = half // rank
    message = jax.ShapeDtypeStruct((2 * count, part, rank), BF16)
    deal = jax.ShapeDtypeStruct((chunk, rows.shape[1]), BF16)
    return pl.pallas_call(
        functools.partial(pack_kernel, deals),
        grid_spec=pltpu.PrefetchScalarGridSpec(
            num_scalar_prefetch=1,
            grid=(1,),
            in_specs=[ANY] * 3,
            out_specs=[ANY] * (2 + deals),
            scratch_shapes=[
                pltpu.VMEM((2,) + message.shape, BF16),
                pltpu.VMEM((deals,) + deal.shape, BF16),
                pltpu.SemaphoreType.DMA((2 * (2 + count) + 2 * deals,)),
            ],
        ),
        out_shape=[message] * 2 + [deal] * deals,
        name="pack",
    )(meta, down.reshape(2, count, part, rank), up, rows)


def room_kernel(*refs):
    del refs


def room_call(shapes):
    return pl.pallas_call(
        room_kernel, out_specs=[ANY] * len(shapes), out_shape=shapes, name="room"
    )()


def stage_kernel(plan, slot, held, firsts, *refs):
    count = len(plan)
    meta_ref, gain_ref, dealt_ref, top_ref, grad_ref = refs[:5]
    arrived = dict(zip(held, refs[5 : 5 + len(held)]))
    pieces = refs[5 + len(held) : 5 + len(held) + count]
    rest = refs[5 + len(held) + count :]
    rest = rest[3 + firsts :]
    packet_ref, pairs_ref, saved_ref, sums_ref = rest[:4]
    first_ref = rest[4] if firsts else None
    (
        down_s,
        up_s,
        packet_s,
        out_s,
        saved_s,
        sums_s,
        weight_sem,
        packet_sem,
        out_sem,
    ) = rest[4 + firsts :]
    rows, wide = packet_s.shape
    width = wide // 2
    half = width // 2
    spans, rank = up_s.shape[1], up_s.shape[2]
    per = down_s.shape[1] // spans
    source, micro = meta_ref[slot, 0], meta_ref[slot, 1]

    @pl.when(meta_ref[slot, 2] == 1)
    def _():
        place = pl.ds(pl.multiple_of(micro * rows, rows), rows)
        before = pl.ds(pl.multiple_of(jnp.maximum(micro - 1, 0) * rows, rows), rows)
        pair_s = packet_s.at[:, pl.ds(0, width)]
        grad_copy = pltpu.make_async_copy(
            grad_ref.at[place], packet_s.at[:, pl.ds(width, width)], packet_sem.at[1]
        )
        options = [
            (
                jnp.logical_and(source == 0, micro == 0),
                [pltpu.make_async_copy(dealt_ref, pair_s, packet_sem.at[0]), grad_copy],
            ),
            (
                jnp.logical_and(source == 0, micro > 0),
                [pltpu.make_async_copy(top_ref.at[before], pair_s, packet_sem.at[0]), grad_copy],
            ),
        ]
        for kind, ref in arrived.items():
            copy = pltpu.make_async_copy(ref, packet_s, packet_sem.at[1 + kind])
            options.append((source == kind, [copy]))

        def each_option(action):
            for chosen, copies in options:

                @pl.when(chosen)
                def _():
                    for copy in copies:
                        action(copy)

        def each_piece(action, low, high, wanted=None):
            for number, (ref, (branch_field, place_field, valid_field)) in enumerate(
                zip(pieces, plan)
            ):
                index, spot = meta_ref[slot, branch_field], meta_ref[slot, place_field]
                part = ref.shape[1]
                start = pl.multiple_of(spot * part, part)
                copies = [
                    pltpu.make_async_copy(
                        ref.at[pl.ds(0, spans)],
                        down_s.at[index, pl.ds(spot * spans, spans)],
                        weight_sem.at[2 * number],
                    ),
                    pltpu.make_async_copy(
                        ref.at[pl.ds(spans, spans)],
                        up_s.at[index, :, pl.ds(start, part)],
                        weight_sem.at[2 * number + 1],
                    ),
                ]
                chosen = meta_ref[slot, valid_field] == 1
                if wanted is not None:
                    chosen = jnp.logical_and(chosen, index == wanted)

                @pl.when(chosen)
                def _():
                    for copy in copies[low:high]:
                        action(copy)

        each_option(lambda copy: copy.start())
        each_piece(lambda copy: copy.start(), 0, 2, 1)
        each_piece(lambda copy: copy.start(), 0, 2, 0)
        each_option(lambda copy: copy.wait())

        def branch(index, values_ref, start, cot, base, less, goal, plus, result):
            def span(c):
                return slice(c * rank, (c + 1) * rank)

            def take(ref, origin, c):
                return ref[:, origin + c * rank : origin + (c + 1) * rank].astype(F32)

            total = None
            for c in range(spans):
                values = take(values_ref, start, c)
                term = jnp.sum(values * values, axis=-1, keepdims=True)
                total = term if total is None else total + term
            inverse = lax.rsqrt(total / half + EPS)
            for c in range(spans):
                gain = gain_ref[index : index + 1, span(c)].astype(F32)
                scaled = (take(values_ref, start, c) * inverse * gain).astype(BF16)
                saved_s[:, base + c * rank : base + (c + 1) * rank] = scaled
            each_piece(lambda copy: copy.wait(), 0, 2, index)
            down = down_s[index].reshape(half, rank)
            pre = dot(saved_s[:, base : base + half], down)
            sigma = jax.nn.sigmoid(pre)
            hidden = (pre * sigma).astype(BF16)
            saved_s[:, base + half : base + half + rank] = hidden
            grad_hidden = None
            for c in range(spans):
                term = dot_nt(cot(c), up_s[index, c])
                grad_hidden = term if grad_hidden is None else grad_hidden + term
            slope = sigma * (1.0 + pre * (1.0 - sigma))
            grad_pre = (grad_hidden * slope).astype(BF16)
            saved_s[:, base + half + rank : base + half + 2 * rank] = grad_pre
            mean = jnp.sum(grad_pre.astype(F32) * pre, axis=-1, keepdims=True) / half
            for c in range(spans):
                output = dot(hidden, up_s[index, c])
                out_s[:, goal + c * rank : goal + (c + 1) * rank] = (
                    take(packet_s, less, c) - output
                ).astype(BF16)
            for c in range(spans):
                part = down_s[index, c * per : (c + 1) * per].reshape(rank, rank)
                grad_scaled = dot_nt(grad_pre, part)
                normed = take(values_ref, start, c) * inverse
                sums_s[index : index + 1, span(c)] = jnp.sum(
                    grad_scaled * normed, axis=0, keepdims=True
                )
                gain = gain_ref[index : index + 1, span(c)].astype(F32)
                back = inverse * (grad_scaled * gain - normed * mean)
                out_s[:, result + c * rank : result + (c + 1) * rank] = (
                    take(packet_s, plus, c) + back
                ).astype(BF16)

        block = half + 2 * rank
        saved_s[:, 2 * block :] = packet_s[:, width + half :]
        branch(
            1,
            packet_s,
            0,
            lambda c: packet_s[:, width + half + c * rank : width + half + (c + 1) * rank],
            block,
            half,
            half,
            width,
            width,
        )
        branch(
            0,
            out_s,
            half,
            lambda c: out_s[:, width + c * rank : width + (c + 1) * rank],
            0,
            0,
            0,
            width + half,
            width + half,
        )
        grad_s = out_s.at[:, pl.ds(width, width)]
        outs = [(out_s, packet_ref), (grad_s, pairs_ref.at[place]), (saved_s, saved_ref.at[place])]
        outs.append((sums_s, sums_ref.at[micro]))
        outs = [
            pltpu.make_async_copy(origin, goal, out_sem.at[number])
            for number, (origin, goal) in enumerate(outs)
        ]
        for copy in outs:
            copy.start()
        if firsts:
            first_copy = pltpu.make_async_copy(grad_s, first_ref, out_sem.at[4])

            @pl.when(micro == 0)
            def _():
                first_copy.start()
                first_copy.wait()

        for copy in outs:
            copy.wait()


def stage_call(slot, meta, gains, dealt, top, grad, arrived, pieces, plan, state):
    rows, width = dealt.shape
    half = width // 2
    rank = pieces[0].shape[2]
    parts = rank // pieces[0].shape[1]
    held = tuple(arrived)
    firsts = len(state) - 3
    n_in = 5 + len(held) + len(pieces)
    inner = [pl.BlockSpec(memory_space=pltpu.VMEM)] * len(held)
    packet, *state = pl.pallas_call(
        functools.partial(stage_kernel, plan, slot, held, firsts),
        grid_spec=pltpu.PrefetchScalarGridSpec(
            num_scalar_prefetch=1,
            grid=(1,),
            in_specs=[pl.BlockSpec(gains.shape, lambda *_: (0, 0))]
            + [ANY] * 3
            + inner
            + [ANY] * (len(pieces) + len(state)),
            out_specs=[ANY] * (1 + len(state)),
            scratch_shapes=[
                pltpu.VMEM((2, parts * half // rank, rank // parts, rank), BF16),
                pltpu.VMEM((2, half // rank, rank, rank), BF16),
                pltpu.VMEM((rows, 2 * width), BF16),
                pltpu.VMEM((rows, 2 * width), BF16),
                pltpu.VMEM((rows, state[1].shape[1]), BF16),
                pltpu.VMEM((8, half), F32),
                pltpu.SemaphoreType.DMA((2 * len(pieces),)),
                pltpu.SemaphoreType.DMA((4,)),
                pltpu.SemaphoreType.DMA((5,)),
            ],
        ),
        out_shape=[jax.ShapeDtypeStruct((rows, 2 * width), BF16)]
        + [jax.ShapeDtypeStruct(a.shape, a.dtype) for a in state],
        input_output_aliases={n_in + i: 1 + i for i in range(len(state))},
        cost_estimate=pl.CostEstimate(
            flops=16 * 2 * rows * half * rank, transcendentals=0, bytes_accessed=8 * rows * width
        ),
        name="stage",
    )(meta, gains, dealt, top, grad, *arrived.values(), *pieces, *state)
    return packet, state


def weight_kernel(fields, meta_ref, saved_ref, first_ref, sums_ref, *refs):
    outs = refs[: len(fields)]
    down_s, up_s, gain_s, sem = refs[len(fields) :]
    spans, rank = up_s.shape[1], up_s.shape[2]
    half = spans * rank
    part = outs[0].shape[1]
    parts = rank // part
    block = half + 2 * rank
    copies = []

    def send(source, goal):
        copies.append(pltpu.make_async_copy(source, goal, sem.at[len(copies)]))
        copies[-1].start()

    spots = [meta_ref[0, field] for field in fields]
    for index in (1, 0):
        base = block * index
        scaled = saved_ref[:, base : base + half]
        hidden = saved_ref[:, base + half : base + half + rank]
        grad_pre = saved_ref[:, base + half + rank : base + block]
        cot = saved_ref[:, 2 * block : 2 * block + half] if index == 1 else first_ref[...]
        for c in range(spans):
            up_s[index, c] = dot_tn(hidden, cot[:, c * rank : (c + 1) * rank]).astype(BF16)
        for out, spot in zip(outs, spots):
            start = pl.multiple_of(spot * part, part)
            send(
                up_s.at[index, :, pl.ds(start, part)],
                out.at[pl.ds((2 * index + 1) * spans, spans)],
            )
        down_s[index] = dot_tn(scaled, grad_pre).astype(BF16).reshape(down_s.shape[1:])
        for out, spot in zip(outs, spots):
            send(
                down_s.at[index, pl.ds(spot * spans, spans)],
                out.at[pl.ds(2 * index * spans, spans)],
            )
    gain_s[...] = jnp.zeros_like(gain_s)
    for number, (out, spot) in enumerate(zip(outs, spots)):
        size = half // parts
        for row, low in enumerate(range(0, size, rank)):
            high = min(low + rank, size)
            start = pl.multiple_of(spot * size + low, 128)
            gain = jnp.sum(sums_ref[:, :, pl.ds(start, high - low)], axis=0)
            gain_s[number, 0, 8 * row : 8 * row + 8, 0 : high - low] = gain.astype(BF16)
        send(gain_s.at[number], out.at[pl.ds(4 * spans, 1)])
    for copy in copies:
        copy.wait()


def weight_call(meta, saved, pairs, sums, fields, parts, half, rank):
    total = saved.shape[0]
    spans, part = half // rank, rank // parts
    return pl.pallas_call(
        functools.partial(weight_kernel, fields),
        grid_spec=pltpu.PrefetchScalarGridSpec(
            num_scalar_prefetch=1,
            grid=(1,),
            in_specs=[
                pl.BlockSpec(saved.shape, lambda *_: (0, 0)),
                pl.BlockSpec((total, half), lambda *_: (0, 0)),
                pl.BlockSpec(sums.shape, lambda *_: (0, 0, 0)),
            ],
            out_specs=[ANY] * len(fields),
            scratch_shapes=[
                pltpu.VMEM((2, parts * spans, part, rank), BF16),
                pltpu.VMEM((2, spans, rank, rank), BF16),
                pltpu.VMEM((len(fields), 1, part, rank), BF16),
                pltpu.SemaphoreType.DMA((5 * len(fields),)),
            ],
        ),
        out_shape=[jax.ShapeDtypeStruct((4 * spans + 1, part, rank), BF16)] * len(fields),
        name="weight",
    )(meta, saved, pairs, sums)


def total_kernel(count, scale, *refs):
    messages, (down_ref, up_ref, gain_ref) = refs[:count], refs[count:]
    spans = up_ref.shape[2] // messages[0].shape[2]
    rank = messages[0].shape[2]

    def total(*where):
        out = messages[0][where].astype(F32)
        for message in messages[1:]:
            out += message[where].astype(F32)
        return out * scale

    for index in range(2):
        base = 2 * index * spans
        down_ref[index] = total(slice(base, base + spans))
        for c in range(spans):
            up_ref[index, :, c * rank : (c + 1) * rank] = total(base + spans + c)
    size = gain_ref.shape[1]
    for row, low in enumerate(range(0, size, rank)):
        high = min(low + rank, size)
        block = total(4 * spans)
        gain_ref[:, low:high] = block[8 * row : 8 * row + 2, 0 : high - low]


def total_call(messages, scale, half):
    _, part, rank = messages[0].shape
    spans = half // rank
    down, up, gain = pl.pallas_call(
        functools.partial(total_kernel, len(messages), scale),
        out_shape=[
            jax.ShapeDtypeStruct((2, spans, part, rank), F32),
            jax.ShapeDtypeStruct((2, part, half), F32),
            jax.ShapeDtypeStruct((2, spans * part), F32),
        ],
        name="total",
    )(*messages)
    return down.reshape(2, spans * part, rank), up, gain


def shards(top_pair, kept, teacher, down_proj, up_proj, gains, head_proj, head_gain, head_out):
    devices = lax.axis_size("dp")
    sections = lax.axis_size("section")
    own = lax.axis_index("dp")
    section = lax.axis_index("section")
    side = lax.axis_index("groups")
    slots, width = top_pair.shape
    half, rank = width // 2, down_proj.shape[3]
    unit = slots // LONG
    chunk = (LONG - 1) * unit // QUAD
    rows_total = unit + chunk
    micros = rows_total // chunk
    quads = devices // QUAD
    place = own % QUAD
    top = sections - 1
    via = 1 if sections == 4 else top
    direct = devices == QUAD and lax.axis_size("groups") == 2 and sections == 4
    parts = QUAD if direct else 1

    def shift_pairs(k, lane=None):
        out = []
        for q in range(quads):
            for i in range(QUAD):
                source, goal = QUAD * q + i, QUAD * q + (i + k) % QUAD
                if lane is not None:
                    source, goal = source * sections + lane, goal * sections + lane
                out.append((source, goal))
        return out

    ids = jnp.arange(devices, dtype=jnp.int32)
    is_longest = jnp.logical_and(ids // QUAD == own // QUAD, kept > unit)
    longest = jnp.sum(jnp.where(is_longest, ids % QUAD, 0))
    mine = 1 - side if direct else jnp.zeros((), jnp.int32)
    is_top = section == top

    offsets = {top: 0}
    for s in range(top, 0, -1):
        offsets[s - 1] = offsets[s] + (1 if s % 2 == 1 else 2)
    count = micros + offsets[0]
    behind = jnp.take(jnp.array([offsets[s] for s in range(sections)], jnp.int32), section)
    source = jnp.where(is_top, 0, jnp.where(section % 2 == 0, 1, 2))
    step = jnp.arange(count, dtype=jnp.int32) - behind
    last = parts - 1
    fields = [
        source,
        jnp.clip(step, 0, micros - 1),
        jnp.logical_and(step >= 0, step < micros),
        mine,
        is_top,
        own,
        1 - mine,
        own if direct else 0,
    ]
    fields += [(own - k) % parts for k in range(QUAD)]
    fields += [
        jnp.clip(own - 1, 0, last),
        jnp.clip(own + 1, 0, last),
        (own + 2) % parts,
        jnp.clip(last - own, 0, last),
        own >= 1,
        own <= 2,
        jnp.logical_or(own == 0, own == 3),
        1,
    ]
    fields += [unit + chunk * ((place + k) % QUAD) for k in range(1, QUAD)]
    meta = jnp.stack(
        [jnp.broadcast_to(jnp.asarray(f).astype(jnp.int32), (count,)) for f in fields], axis=1
    )

    if direct:
        down, up = down_proj[0], up_proj[0]
    else:
        down = lax.all_gather(down_proj[0], "dp", axis=1, tiled=True)
        up = lax.all_gather(up_proj[0], "dp", axis=1, tiled=True)
    mine_msg, other_msg, *deals = pack_call(meta, down, up, top_pair, QUAD - 1, chunk)
    pieces, plan = [mine_msg, other_msg], [(3, 7, 19), (6, 7, 19)]

    dealt = lax.dynamic_slice_in_dim(top_pair, unit + chunk * place, chunk)
    for k, deal in enumerate(deals, 1):
        other = lax.ppermute(deal, ("dp", "section"), shift_pairs(k, via))
        dealt = jnp.where((place - k) % QUAD == longest, other, dealt)
    if direct:
        head_pieces = [head_proj]
        for k in range(1, QUAD):
            head_pieces.append(lax.ppermute(head_proj, ("dp", "section"), shift_pairs(k, top)))
        dealt = lax.ppermute(dealt, "section", [(via, top)])

        def along(array, pairs):
            return lax.ppermute(array, "dp", pairs)

        def across(array, valid):
            pairs = [(QUAD * g + i, QUAD * (1 - g) + i) for g in (0, 1) for i in valid]
            return lax.ppermute(array, ("groups", "dp"), pairs)

        right = along(mine_msg, [(0, 1), (1, 2), (2, 3)])
        left = along(mine_msg, [(1, 0), (2, 1), (3, 2)])
        far = along(mine_msg, [(0, 2), (1, 3), (2, 0), (3, 1)])
        relay = along(far, [(1, 0), (2, 3)])
        for piece, place_field, valid_field, valid in (
            (right, 12, 16, (1, 2, 3)),
            (left, 13, 17, (0, 1, 2)),
            (far, 14, 19, (0, 1, 2, 3)),
            (relay, 15, 18, (0, 3)),
        ):
            pieces += [piece, across(piece, valid)]
            plan += [(3, place_field, valid_field), (6, place_field, valid_field)]
    else:
        head_pieces = [lax.all_gather(head_proj, "dp", axis=0, tiled=True)]

    gain_row, out_row = head_gain[None], head_out[None]
    coef = score_call(meta, kept, teacher, top_pair, gain_row, out_row, head_pieces, unit)
    far_coef = coef
    for k in range(1, QUAD):
        other = lax.ppermute(coef, ("dp", "section"), shift_pairs(k, top))
        far_coef = jnp.where((place - k) % QUAD == longest, other, far_coef)
    grad = head_call(meta, dealt, top_pair, far_coef, coef, gain_row, out_row, head_pieces, rows_total)

    pairs, saved, sums, first = room_call(
        [
            jax.ShapeDtypeStruct((rows_total, width), BF16),
            jax.ShapeDtypeStruct((rows_total, 2 * (half + 2 * rank) + half), BF16),
            jax.ShapeDtypeStruct((micros, 8, half), F32),
            jax.ShapeDtypeStruct((chunk, width), BF16),
        ]
    )
    state = [pairs, saved, sums, first]
    near, far_in = {}, {}
    for slot in range(count):
        arrived = {1: near.get(slot - 1), 2: far_in.get(slot - 2)}
        arrived = {kind: array for kind, array in arrived.items() if array is not None}
        packet, state = stage_call(
            slot, meta, gains[0], dealt, top_pair, grad, arrived, pieces, plan, state
        )
        live = [s for s in range(1, sections) if 0 <= slot - offsets[s] < micros]
        for table, odd in ((near, 1), (far_in, 0)):
            hops = [(s, s - 1) for s in live if s % 2 == odd]
            if hops:
                table[slot] = lax.ppermute(packet, "section", hops)
        if slot == offsets[0]:
            piece = state.pop()
    pairs, saved, sums = state

    returned = [piece] + [lax.ppermute(piece, "dp", shift_pairs(k)) for k in range(1, QUAD)]
    is_long = longest == place
    parts_out = [pairs[chunk:]]
    for j in range(QUAD):
        value = returned[0]
        for k in range(1, QUAD):
            value = jnp.where((place - k) % QUAD == j, returned[k], value)
        parts_out.append(jnp.where(is_long, value, 0).astype(BF16))
    grads_out = jnp.concatenate(parts_out, axis=0)

    if direct:
        own_w, right_w, left_w, far_w, relay_w = weight_call(
            meta, saved, pairs, sums, (7, 13, 12, 14, 15), parts, half, rank
        )
        handed = along(relay_w, [(0, 1), (3, 2)])
        from_left = along(right_w, [(0, 1), (1, 2), (2, 3)])
        from_right = along(left_w, [(1, 0), (2, 1), (3, 2)])
        far_w = (far_w.astype(F32) + handed.astype(F32)).astype(BF16)
        from_far = along(far_w, [(0, 2), (1, 3), (2, 0), (3, 1)])
        messages = [own_w, from_left, from_right, from_far]
        down_sum, up_sum, gain_sum = total_call(messages, 1.0 / devices, half)
    else:
        (whole,) = weight_call(meta, saved, pairs, sums, (7,), parts, half, rank)
        down_sum, up_sum, gain_sum = total_call([whole], 1.0 / devices, half)
        scatter = functools.partial(lax.psum_scatter, axis_name="dp", scatter_dimension=1, tiled=True)
        down_sum, up_sum, gain_sum = scatter(down_sum), scatter(up_sum), scatter(gain_sum)
    return grads_out[None], down_sum[None], up_sum[None], gain_sum[None]


def solution(mesh):
    in_specs = (
        P(("groups", "dp"), None),
        P("groups"),
        P("groups"),
        P("section", None, "dp", None),
        P("section", None, "dp", None),
        P("section", None, None),
        P("dp", None),
        P(),
        P(),
    )
    out_specs = (
        P("section", ("groups", "dp"), None),
        P(("groups", "section"), None, "dp", None),
        P(("groups", "section"), None, "dp", None),
        P(("groups", "section"), None, "dp"),
    )
    return jax.shard_map(shards, mesh=mesh, in_specs=in_specs, out_specs=out_specs, check_vma=False)
```

```python
import functools

import jax
import jax.numpy as jnp
from jax import lax
from jax.experimental import pallas as pl
from jax.experimental.pallas import tpu as pltpu
from jax.sharding import PartitionSpec as P


EPS = 1e-06
LOSS_SCALE = 4096.0
FIXED_POINT = 256.0
QUAD = 4
LONG = 3
F32 = jnp.float32
BF16 = jnp.bfloat16
ANY = pl.BlockSpec(memory_space=pl.ANY)
HBM = pl.BlockSpec(memory_space=pltpu.HBM)
VMEM = pl.BlockSpec(memory_space=pltpu.VMEM)


def dot(left, right):
    return jnp.dot(left, right, preferred_element_type=F32)


def dot_nt(left, right):
    return lax.dot_general(left, right, (((1,), (1,)), ((), ())), preferred_element_type=F32)


def dot_tn(left, right):
    return lax.dot_general(left, right, (((0,), (0,)), ((), ())), preferred_element_type=F32)


def norm_parts(rows):
    values = rows.astype(F32)
    inverse = lax.rsqrt(jnp.mean(values * values, axis=-1, keepdims=True) + EPS)
    return values * inverse, inverse


def head_logits(normed, gain_ref, scaled_ref, meta_ref, pieces):
    scaled_ref[...] = (normed * gain_ref[...].astype(F32)).astype(BF16)
    part = pieces[0].shape[0]
    total = None
    for k, piece in enumerate(pieces):
        start = pl.multiple_of(meta_ref[0, 8 + k] * part, part)
        term = dot(scaled_ref[:, pl.ds(start, part)], piece[...])
        total = term if total is None else total + term
    return total


def score_kernel(count, unit, meta_ref, kept_ref, teacher_ref, rows_ref, gain_ref, out_ref, *rest):
    pieces, (coef_ref, scaled_ref) = rest[:count], rest[count:]
    step = pl.program_id(0)
    kept = kept_ref[meta_ref[0, 5]]

    @pl.when(step == 0)
    def _():
        coef_ref[...] = jnp.zeros_like(coef_ref)

    @pl.when(jnp.logical_and(meta_ref[0, 4] == 1, step * unit < kept))
    def _():
        normed, _ = norm_parts(rows_ref[...])
        logits = head_logits(normed, gain_ref, scaled_ref, meta_ref, pieces)
        scores = jax.nn.silu(logits) * out_ref[...].astype(F32)
        place = lax.broadcasted_iota(jnp.int32, scores.shape, 0) + step * unit
        scores = jnp.where(place < kept, scores, 0.0)
        coef_ref[...] += jnp.broadcast_to(jnp.sum(scores), coef_ref.shape)

    @pl.when(step == pl.num_programs(0) - 1)
    def _():
        counts = jnp.full(coef_ref.shape, kept, jnp.int32).astype(F32)
        target = jnp.full(coef_ref.shape, teacher_ref[meta_ref[0, 5]], jnp.int32).astype(F32)
        score = coef_ref[...] / counts
        coef_ref[...] = 2.0 * LOSS_SCALE * (score - target / FIXED_POINT) / counts


def score_call(meta, kept, teacher, rows, gain, out, pieces, unit):
    slots, width = rows.shape
    keep = lambda *_: (0, 0)
    return pl.pallas_call(
        functools.partial(score_kernel, len(pieces), unit),
        grid_spec=pltpu.PrefetchScalarGridSpec(
            num_scalar_prefetch=3,
            grid=(slots // unit,),
            in_specs=[
                pl.BlockSpec((unit, width), lambda i, *_: (i, 0)),
                pl.BlockSpec(gain.shape, keep),
                pl.BlockSpec(out.shape, keep),
            ]
            + [pl.BlockSpec(p.shape, keep) for p in pieces],
            out_specs=pl.BlockSpec((8, 128), keep),
            scratch_shapes=[pltpu.VMEM((unit, width), BF16)],
        ),
        out_shape=jax.ShapeDtypeStruct((8, 128), F32),
        cost_estimate=pl.CostEstimate(
            flops=2 * slots * width * out.shape[1],
            transcendentals=slots * out.shape[1],
            bytes_accessed=12 * slots * width,
        ),
        compiler_params=pltpu.CompilerParams(vmem_limit_bytes=24 << 20),
        name="score",
    )(meta, kept, teacher, rows, gain, out, *pieces)


def head_kernel(count, meta_ref, dealt_ref, rows_ref, far_ref, own_ref, gain_ref, out_ref, *rest):
    pieces, (packet_ref, scaled_ref, normal_ref) = rest[:count], rest[count:]
    step = pl.program_id(0)

    @pl.when(meta_ref[0, 4] == 1)
    def _():
        rows = jnp.where(step == 0, dealt_ref[...], rows_ref[...])
        width = rows.shape[1]
        packet_ref[:, :width] = rows
        normed, inverse = norm_parts(rows)
        normal_ref[...] = normed
        logits = head_logits(normed, gain_ref, scaled_ref, meta_ref, pieces)
        coef = jnp.where(step == 0, far_ref[0:1, :], own_ref[0:1, :])
        sigma = jax.nn.sigmoid(logits)
        slope = sigma * (1.0 + logits * (1.0 - sigma))
        grad = (coef * out_ref[...].astype(F32) * slope).astype(BF16)
        part = pieces[0].shape[0]
        mean = jnp.zeros_like(inverse)
        spans = []
        for k, piece in enumerate(pieces):
            start = pl.multiple_of(meta_ref[0, 8 + k] * part, part)
            span = pl.ds(start, part)
            weighted = dot_nt(grad, piece[...]) * gain_ref[:, span].astype(F32)
            mean += jnp.sum(normal_ref[:, span] * weighted, axis=-1, keepdims=True)
            spans.append((span, weighted))
        mean = mean / normed.shape[1]
        for k, (span, weighted) in enumerate(spans):
            start = pl.multiple_of(meta_ref[0, 8 + k] * part + width, part)
            back = inverse * (weighted - normal_ref[:, span] * mean)
            packet_ref[:, pl.ds(start, part)] = back.astype(BF16)


def head_call(meta, dealt, rows, far, own, gain, out, pieces, total):
    block, width = dealt.shape
    keep = lambda *_: (0, 0)
    return pl.pallas_call(
        functools.partial(head_kernel, len(pieces)),
        grid_spec=pltpu.PrefetchScalarGridSpec(
            num_scalar_prefetch=1,
            grid=(total // block,),
            in_specs=[
                pl.BlockSpec((block, width), keep),
                pl.BlockSpec((block, width), lambda i, *_: (jnp.maximum(i - 1, 0), 0)),
                pl.BlockSpec((8, 128), keep),
                pl.BlockSpec((8, 128), keep),
                pl.BlockSpec(gain.shape, keep),
                pl.BlockSpec(out.shape, keep),
            ]
            + [pl.BlockSpec(p.shape, keep) for p in pieces],
            out_specs=pl.BlockSpec((block, 2 * width), lambda i, *_: (i, 0)),
            scratch_shapes=[pltpu.VMEM((block, width), BF16), pltpu.VMEM((block, width), F32)],
        ),
        out_shape=jax.ShapeDtypeStruct((total, 2 * width), BF16),
        cost_estimate=pl.CostEstimate(
            flops=4 * total * width * out.shape[1],
            transcendentals=total * out.shape[1],
            bytes_accessed=24 * total * width,
        ),
        compiler_params=pltpu.CompilerParams(vmem_limit_bytes=24 << 20),
        name="head",
    )(meta, dealt, rows, far, own, gain, out, *pieces)


def pack_kernel(deals, meta_ref, down_ref, up_ref, rows_ref, *refs):
    outs, (message_s, deal_s, sem) = refs[: 2 + deals], refs[2 + deals :]
    count, rank = outs[0].shape[0] // 2, outs[0].shape[2]
    copies = []

    def copy(source, goal):
        copies.append(pltpu.make_async_copy(source, goal, sem.at[len(copies)]))
        copies[-1].start()

    for number, field in enumerate((3, 6)):
        index = meta_ref[0, field]
        copy(down_ref.at[index], message_s.at[number, pl.ds(0, count)])
        for c in range(count):
            copy(up_ref.at[index, :, pl.ds(c * rank, rank)], message_s.at[number, count + c])
    for k in range(deals):
        rows = deal_s.shape[1]
        start = pl.multiple_of(meta_ref[0, 20 + k], rows)
        copy(rows_ref.at[pl.ds(start, rows)], deal_s.at[k])
    each = 1 + count
    for number in range(2):
        for one in copies[number * each : (number + 1) * each]:
            one.wait()
        copy(message_s.at[number], outs[number])
    for k in range(deals):
        copies[2 * each + k].wait()
        copy(deal_s.at[k], outs[2 + k])
    for one in copies[2 * each + deals :]:
        one.wait()


def pack_call(meta, down, up, rows, deals, chunk):
    part, half = up.shape[1:]
    rank = down.shape[2]
    count = half // rank
    message = jax.ShapeDtypeStruct((2 * count, part, rank), BF16)
    deal = jax.ShapeDtypeStruct((chunk, rows.shape[1]), BF16)
    return pl.pallas_call(
        functools.partial(pack_kernel, deals),
        grid_spec=pltpu.PrefetchScalarGridSpec(
            num_scalar_prefetch=1,
            grid=(1,),
            in_specs=[HBM] * 3,
            out_specs=[HBM] * (2 + deals),
            scratch_shapes=[
                pltpu.VMEM((2,) + message.shape, BF16),
                pltpu.VMEM((deals,) + deal.shape, BF16),
                pltpu.SemaphoreType.DMA((2 * (2 + count) + 2 * deals,)),
            ],
        ),
        out_shape=[message] * 2 + [deal] * deals,
        compiler_params=pltpu.CompilerParams(vmem_limit_bytes=60 << 20),
        name="pack",
    )(meta, down.reshape(2, count, part, rank), up, rows)


def assemble_kernel(plan, meta_ref, *refs):
    pieces, (down_ref, up_ref, sem) = refs[: len(plan)], refs[len(plan) :]
    spans = up_ref.shape[1]

    def each(action):
        for number, (ref, (branch_field, place_field, valid_field)) in enumerate(zip(pieces, plan)):
            index, spot = meta_ref[0, branch_field], meta_ref[0, place_field]
            part = ref.shape[1]
            start = pl.multiple_of(spot * part, part)
            copies = [
                pltpu.make_async_copy(
                    ref.at[pl.ds(0, spans)],
                    down_ref.at[index, pl.ds(spot * spans, spans)],
                    sem.at[2 * number],
                ),
                pltpu.make_async_copy(
                    ref.at[pl.ds(spans, spans)],
                    up_ref.at[index, :, pl.ds(start, part)],
                    sem.at[2 * number + 1],
                ),
            ]

            @pl.when(meta_ref[0, valid_field] == 1)
            def _():
                for copy in copies:
                    action(copy)

    each(lambda copy: copy.start())
    each(lambda copy: copy.wait())


def assemble_call(meta, pieces, plan, half):
    rank = pieces[0].shape[2]
    part = pieces[0].shape[1]
    return pl.pallas_call(
        functools.partial(assemble_kernel, plan),
        grid_spec=pltpu.PrefetchScalarGridSpec(
            num_scalar_prefetch=1,
            grid=(1,),
            in_specs=[ANY] * len(pieces),
            out_specs=[VMEM] * 2,
            scratch_shapes=[pltpu.SemaphoreType.DMA((2 * len(pieces),))],
        ),
        out_shape=[
            jax.ShapeDtypeStruct((2, half // part, part, rank), BF16),
            jax.ShapeDtypeStruct((2, half // rank, rank, rank), BF16),
        ],
        compiler_params=pltpu.CompilerParams(vmem_limit_bytes=8 << 20),
        name="assemble",
    )(meta, *pieces)


def output_kernel(unit, meta_ref, kept_ref, pairs_ref, *refs):
    pieces, (out_ref, zero_s, sem) = refs[:QUAD], refs[QUAD:]
    chunk = pieces[0].shape[0]
    own = pltpu.make_async_copy(
        pairs_ref.at[pl.ds(chunk, unit)], out_ref.at[pl.ds(0, unit)], sem.at[QUAD]
    )
    own.start()
    long = kept_ref[meta_ref[0, 5]] > unit
    zero_s[...] = jnp.zeros_like(zero_s)
    for k, piece in enumerate(pieces):
        start = pl.multiple_of(meta_ref[0, 23 + k], chunk)
        goal = out_ref.at[pl.ds(start, chunk)]

        @pl.when(long)
        def _():
            pltpu.make_async_copy(piece, goal, sem.at[k]).start()

        @pl.when(jnp.logical_not(long))
        def _():
            pltpu.make_async_copy(zero_s, goal, sem.at[k]).start()

    for k in range(QUAD):
        start = pl.multiple_of(meta_ref[0, 23 + k], chunk)
        pltpu.make_async_copy(zero_s, out_ref.at[pl.ds(start, chunk)], sem.at[k]).wait()
    own.wait()


def output_call(meta, kept, pairs, pieces, slots):
    chunk, width = pieces[0].shape
    return pl.pallas_call(
        functools.partial(output_kernel, slots // LONG),
        grid_spec=pltpu.PrefetchScalarGridSpec(
            num_scalar_prefetch=2,
            grid=(1,),
            in_specs=[ANY] * (1 + len(pieces)),
            out_specs=ANY,
            scratch_shapes=[
                pltpu.VMEM((chunk, width), BF16),
                pltpu.SemaphoreType.DMA((QUAD + 1,)),
            ],
        ),
        out_shape=jax.ShapeDtypeStruct((slots, width), BF16),
        compiler_params=pltpu.CompilerParams(vmem_limit_bytes=4 << 20),
        name="output",
    )(meta, kept, pairs, *pieces)


def stage_kernel(slot, held, firsts, *refs):
    meta_ref, gain_ref, top_ref, down_s, up_s = refs[:5]
    arrived = dict(zip(held, refs[5 : 5 + len(held)]))
    rest = refs[5 + len(held) + (3 + firsts if slot else 0) :]
    packet_ref, pairs_ref, saved_ref, sums_ref = rest[:4]
    first_ref = rest[4] if firsts else None
    packet_s, packet_sem = rest[4 + firsts :]
    rows, wide = packet_s.shape
    width = wide // 2
    half = width // 2
    spans, rank = up_s.shape[1], up_s.shape[2]
    per = down_s.shape[1] // spans
    source, micro = meta_ref[slot, 0], meta_ref[slot, 1]

    @pl.when(meta_ref[slot, 2] == 1)
    def _():
        place = pl.ds(pl.multiple_of(micro * rows, rows), rows)
        options = [
            (
                source == 0,
                [pltpu.make_async_copy(top_ref.at[place], packet_s, packet_sem.at[0])],
            )
        ]
        for kind, ref in arrived.items():
            copy = pltpu.make_async_copy(ref, packet_s, packet_sem.at[1 + kind])
            options.append((source == kind, [copy]))

        def each_option(action):
            for chosen, copies in options:

                @pl.when(chosen)
                def _():
                    for copy in copies:
                        action(copy)

        each_option(lambda copy: copy.start())
        each_option(lambda copy: copy.wait())

        def branch(index, values_ref, start, cot, base, less, goal, plus, result):
            def span(c):
                return slice(c * rank, (c + 1) * rank)

            def take(ref, origin, c):
                return ref[:, origin + c * rank : origin + (c + 1) * rank].astype(F32)

            total = None
            for c in range(spans):
                values = take(values_ref, start, c)
                term = jnp.sum(values * values, axis=-1, keepdims=True)
                total = term if total is None else total + term
            inverse = lax.rsqrt(total / half + EPS)
            for c in range(spans):
                gain = gain_ref[index : index + 1, span(c)].astype(F32)
                scaled = (take(values_ref, start, c) * inverse * gain).astype(BF16)
                saved_ref[place, base + c * rank : base + (c + 1) * rank] = scaled
            down = down_s[index].reshape(half, rank)
            pre = dot(saved_ref[place, base : base + half], down)
            sigma = jax.nn.sigmoid(pre)
            hidden = (pre * sigma).astype(BF16)
            saved_ref[place, base + half : base + half + rank] = hidden
            grad_hidden = None
            for c in range(spans):
                term = dot_nt(cot(c), up_s[index, c])
                grad_hidden = term if grad_hidden is None else grad_hidden + term
            slope = sigma * (1.0 + pre * (1.0 - sigma))
            grad_pre = (grad_hidden * slope).astype(BF16)
            saved_ref[place, base + half + rank : base + half + 2 * rank] = grad_pre
            mean = jnp.sum(grad_pre.astype(F32) * pre, axis=-1, keepdims=True) / half
            for c in range(spans):
                output = dot(hidden, up_s[index, c])
                packet_ref[:, goal + c * rank : goal + (c + 1) * rank] = (
                    take(packet_s, less, c) - output
                ).astype(BF16)
            for c in range(spans):
                part = down_s[index, c * per : (c + 1) * per].reshape(rank, rank)
                grad_scaled = dot_nt(grad_pre, part)
                normed = take(values_ref, start, c) * inverse
                sums_ref[micro, index : index + 1, span(c)] = jnp.sum(
                    grad_scaled * normed, axis=0, keepdims=True
                )
                gain = gain_ref[index : index + 1, span(c)].astype(F32)
                back = inverse * (grad_scaled * gain - normed * mean)
                value = (take(packet_s, plus, c) + back).astype(BF16)
                packet_ref[:, result + c * rank : result + (c + 1) * rank] = value
                low = result - width + c * rank
                pairs_ref[place, low : low + rank] = value

        block = half + 2 * rank
        saved_ref[place, 2 * block :] = packet_s[:, width + half :]
        branch(
            1,
            packet_s,
            0,
            lambda c: packet_s[:, width + half + c * rank : width + half + (c + 1) * rank],
            block,
            half,
            half,
            width,
            width,
        )
        branch(
            0,
            packet_ref,
            half,
            lambda c: packet_ref[:, width + c * rank : width + (c + 1) * rank],
            0,
            0,
            0,
            width + half,
            width + half,
        )
        if firsts:

            @pl.when(micro == 0)
            def _():
                first_ref[...] = packet_ref[:, width:]


def stage_call(slot, meta, gains, top, weights, arrived, state, shapes):
    _, wide = top.shape
    half, rank = wide // 4, weights[0].shape[3]
    rows = shapes[-1].shape[0]
    held = tuple(arrived)
    n_in = 5 + len(held)
    shapes = shapes[: len(state)] if slot else shapes
    packet, *state = pl.pallas_call(
        functools.partial(stage_kernel, slot, held, len(shapes) - 3),
        grid_spec=pltpu.PrefetchScalarGridSpec(
            num_scalar_prefetch=1,
            grid=(1,),
            in_specs=[pl.BlockSpec(gains.shape, lambda *_: (0, 0)), ANY]
            + [VMEM] * (2 + len(held) + len(state)),
            out_specs=[VMEM] * (1 + len(shapes)),
            scratch_shapes=[pltpu.VMEM((rows, wide), BF16), pltpu.SemaphoreType.DMA((4,))],
        ),
        out_shape=[jax.ShapeDtypeStruct((rows, wide), BF16)] + shapes,
        input_output_aliases={n_in + i: 1 + i for i in range(len(state))},
        cost_estimate=pl.CostEstimate(
            flops=16 * 2 * rows * half * rank, transcendentals=0, bytes_accessed=4 * rows * wide
        ),
        compiler_params=pltpu.CompilerParams(vmem_limit_bytes=6 << 20),
        name="stage",
    )(meta, gains, top, *weights, *arrived.values(), *state)
    return packet, state


def weight_kernel(fields, meta_ref, saved_ref, first_ref, sums_ref, *refs):
    outs = refs[: len(fields)]
    down_s, up_s, gain_s, sem = refs[len(fields) :]
    spans, rank = up_s.shape[1], up_s.shape[2]
    half = spans * rank
    part = outs[0].shape[1]
    parts = rank // part
    block = half + 2 * rank
    copies = []

    def send(source, goal):
        copies.append(pltpu.make_async_copy(source, goal, sem.at[len(copies)]))
        copies[-1].start()

    spots = [meta_ref[0, field] for field in fields]
    for index in (1, 0):
        base = block * index
        scaled = saved_ref[:, base : base + half]
        hidden = saved_ref[:, base + half : base + half + rank]
        grad_pre = saved_ref[:, base + half + rank : base + block]
        cot = saved_ref[:, 2 * block : 2 * block + half] if index == 1 else first_ref[:, :half]
        for c in range(spans):
            up_s[index, c] = dot_tn(hidden, cot[:, c * rank : (c + 1) * rank]).astype(BF16)
        for out, spot in zip(outs, spots):
            start = pl.multiple_of(spot * part, part)
            send(
                up_s.at[index, :, pl.ds(start, part)],
                out.at[pl.ds((2 * index + 1) * spans, spans)],
            )
        down_s[index] = dot_tn(scaled, grad_pre).astype(BF16).reshape(down_s.shape[1:])
        for out, spot in zip(outs, spots):
            send(
                down_s.at[index, pl.ds(spot * spans, spans)],
                out.at[pl.ds(2 * index * spans, spans)],
            )
    gain_s[...] = jnp.zeros_like(gain_s)
    for number, (out, spot) in enumerate(zip(outs, spots)):
        size = half // parts
        for row, low in enumerate(range(0, size, rank)):
            high = min(low + rank, size)
            start = pl.multiple_of(spot * size + low, 128)
            gain = jnp.sum(sums_ref[:, :, pl.ds(start, high - low)], axis=0)
            gain_s[number, 0, 8 * row : 8 * row + 8, 0 : high - low] = gain.astype(BF16)
        send(gain_s.at[number], out.at[pl.ds(4 * spans, 1)])
    for copy in copies:
        copy.wait()


def weight_call(meta, saved, pairs, sums, fields, parts, half, rank):
    spans, part = half // rank, rank // parts
    return pl.pallas_call(
        functools.partial(weight_kernel, fields),
        grid_spec=pltpu.PrefetchScalarGridSpec(
            num_scalar_prefetch=1,
            grid=(1,),
            in_specs=[VMEM] * 3,
            out_specs=[HBM] * len(fields),
            scratch_shapes=[
                pltpu.VMEM((2, parts * spans, part, rank), BF16),
                pltpu.VMEM((2, spans, rank, rank), BF16),
                pltpu.VMEM((len(fields), 1, part, rank), BF16),
                pltpu.SemaphoreType.DMA((5 * len(fields),)),
            ],
        ),
        out_shape=[jax.ShapeDtypeStruct((4 * spans + 1, part, rank), BF16)] * len(fields),
        compiler_params=pltpu.CompilerParams(vmem_limit_bytes=16 << 20),
        name="weight",
    )(meta, saved, pairs, sums)


def total_kernel(count, scale, *refs):
    messages, (down_ref, up_ref, gain_ref) = refs[:count], refs[count:]
    spans = up_ref.shape[2] // messages[0].shape[2]
    rank = messages[0].shape[2]

    def total(*where):
        out = messages[0][where].astype(F32)
        for message in messages[1:]:
            out += message[where].astype(F32)
        return out * scale

    for index in range(2):
        base = 2 * index * spans
        down_ref[index] = total(slice(base, base + spans))
        for c in range(spans):
            up_ref[index, :, c * rank : (c + 1) * rank] = total(base + spans + c)
    size = gain_ref.shape[1]
    for row, low in enumerate(range(0, size, rank)):
        high = min(low + rank, size)
        block = total(4 * spans)
        gain_ref[:, low:high] = block[8 * row : 8 * row + 2, 0 : high - low]


def total_call(messages, scale, half):
    _, part, rank = messages[0].shape
    spans = half // rank
    down, up, gain = pl.pallas_call(
        functools.partial(total_kernel, len(messages), scale),
        out_shape=[
            jax.ShapeDtypeStruct((2, spans, part, rank), F32),
            jax.ShapeDtypeStruct((2, part, half), F32),
            jax.ShapeDtypeStruct((2, spans * part), F32),
        ],
        compiler_params=pltpu.CompilerParams(vmem_limit_bytes=24 << 20),
        name="total",
    )(*messages)
    return down.reshape(2, spans * part, rank), up, gain


def device_program(top_pair, kept, teacher, down_proj, up_proj, gains, head_proj, head_gain, head_out):
    devices = lax.axis_size("dp")
    sections = lax.axis_size("section")
    own = lax.axis_index("dp")
    section = lax.axis_index("section")
    side = lax.axis_index("groups")
    slots, width = top_pair.shape
    half, rank = width // 2, down_proj.shape[3]
    unit = slots // LONG
    chunk = (LONG - 1) * unit // QUAD
    rows_total = unit + chunk
    micros = rows_total // chunk
    quads = devices // QUAD
    place = own % QUAD
    top = sections - 1
    via = 1 if sections == 4 else top
    direct = devices == QUAD and lax.axis_size("groups") == 2 and sections == 4
    parts = QUAD if direct else 1

    def shift_pairs(k, lane=None):
        out = []
        for q in range(quads):
            for i in range(QUAD):
                source, goal = QUAD * q + i, QUAD * q + (i + k) % QUAD
                if lane is not None:
                    source, goal = source * sections + lane, goal * sections + lane
                out.append((source, goal))
        return out

    ids = jnp.arange(devices, dtype=jnp.int32)
    is_longest = jnp.logical_and(ids // QUAD == own // QUAD, kept > unit)
    longest = jnp.sum(jnp.where(is_longest, ids % QUAD, 0))
    mine = 1 - side if direct else jnp.zeros((), jnp.int32)
    is_top = section == top

    offsets = {top: 0}
    for s in range(top, 0, -1):
        offsets[s - 1] = offsets[s] + (1 if s % 2 == 1 else 2)
    count = micros + offsets[0]
    behind = (top - section) + (top // 2 - section // 2)
    source = jnp.where(is_top, 0, jnp.where(section % 2 == 0, 1, 2))
    step = jnp.arange(count, dtype=jnp.int32) - behind
    last = parts - 1
    fields = [
        source,
        jnp.clip(step, 0, micros - 1),
        jnp.logical_and(step >= 0, step < micros),
        mine,
        is_top,
        own,
        1 - mine,
        own if direct else 0,
    ]
    fields += [(own - k) % parts for k in range(QUAD)]
    fields += [
        jnp.clip(own - 1, 0, last),
        jnp.clip(own + 1, 0, last),
        (own + 2) % parts,
        jnp.clip(last - own, 0, last),
        own >= 1,
        own <= 2,
        jnp.logical_or(own == 0, own == 3),
        1,
    ]
    fields += [unit + chunk * ((place + k) % QUAD) for k in range(1, QUAD)]
    fields += [unit + chunk * ((place - k) % QUAD) for k in range(QUAD)]
    meta = jnp.stack(
        [jnp.broadcast_to(jnp.asarray(f).astype(jnp.int32), (count,)) for f in fields], axis=1
    )

    if direct:
        down, up = down_proj[0], up_proj[0]
    else:
        down = lax.all_gather(down_proj[0], "dp", axis=1, tiled=True)
        up = lax.all_gather(up_proj[0], "dp", axis=1, tiled=True)
    mine_msg, other_msg, *deals = pack_call(meta, down, up, top_pair, QUAD - 1, chunk)
    pieces, plan = [mine_msg, other_msg], [(3, 7, 19), (6, 7, 19)]

    dealt = lax.dynamic_slice_in_dim(top_pair, unit + chunk * place, chunk)
    for k, deal in enumerate(deals, 1):
        other = lax.ppermute(deal, ("dp", "section"), shift_pairs(k, via))
        dealt = jnp.where((place - k) % QUAD == longest, other, dealt)
    if direct:
        head_pieces = [head_proj]
        for k in range(1, QUAD):
            piece = lax.ppermute(head_proj, ("dp", "section"), shift_pairs(k, via))
            head_pieces.append(lax.ppermute(piece, "section", [(via, top)]))
        dealt = lax.ppermute(dealt, "section", [(via, top)])

        def along(array, pairs):
            return lax.ppermute(array, "dp", pairs)

        def across(array, valid):
            pairs = [(QUAD * g + i, QUAD * (1 - g) + i) for g in (0, 1) for i in valid]
            return lax.ppermute(array, ("groups", "dp"), pairs)

        right = along(mine_msg, [(0, 1), (1, 2), (2, 3)])
        left = along(mine_msg, [(1, 0), (2, 1), (3, 2)])
        far = along(mine_msg, [(0, 2), (1, 3), (2, 0), (3, 1)])
        relay = along(far, [(1, 0), (2, 3)])
        gain_row, out_row = head_gain[None], head_out[None]
        coef = score_call(meta, kept, teacher, top_pair, gain_row, out_row, head_pieces, unit)
        relay, coef = lax.optimization_barrier((relay, coef))
        for piece, place_field, valid_field, valid in (
            (right, 12, 16, (1, 2, 3)),
            (left, 13, 17, (0, 1, 2)),
            (far, 14, 19, (0, 1, 2, 3)),
            (relay, 15, 18, (0, 3)),
        ):
            pieces += [piece, across(piece, valid)]
            plan += [(3, place_field, valid_field), (6, place_field, valid_field)]
    else:
        head_pieces = [lax.all_gather(head_proj, "dp", axis=0, tiled=True)]

    if not direct:
        gain_row, out_row = head_gain[None], head_out[None]
        coef = score_call(meta, kept, teacher, top_pair, gain_row, out_row, head_pieces, unit)
    far_coef = coef
    for k in range(1, QUAD):
        other = lax.ppermute(coef, ("dp", "section"), shift_pairs(k, top))
        far_coef = jnp.where((place - k) % QUAD == longest, other, far_coef)
    packets = head_call(meta, dealt, top_pair, far_coef, coef, gain_row, out_row, head_pieces, rows_total)

    shapes = [
        jax.ShapeDtypeStruct((rows_total, width), BF16),
        jax.ShapeDtypeStruct((rows_total, 2 * (half + 2 * rank) + half), BF16),
        jax.ShapeDtypeStruct((micros, 8, half), F32),
        jax.ShapeDtypeStruct((chunk, width), BF16),
    ]
    state = []
    weights = assemble_call(meta, pieces, plan, half)
    near, far_in = {}, {}
    for slot in range(count):
        arrived = {1: near.get(slot - 1), 2: far_in.get(slot - 2)}
        arrived = {kind: array for kind, array in arrived.items() if array is not None}
        packet, state = stage_call(slot, meta, gains[0], packets, weights, arrived, state, shapes)
        live = [s for s in range(1, sections) if 0 <= slot - offsets[s] < micros]
        for table, odd in ((near, 1), (far_in, 0)):
            hops = [(s, s - 1) for s in live if s % 2 == odd]
            if hops:
                table[slot] = lax.ppermute(packet, "section", hops)
        if slot == offsets[0]:
            piece = state.pop()
    pairs, saved, sums = state

    returned = [piece] + [lax.ppermute(piece, "dp", shift_pairs(k)) for k in range(1, QUAD)]
    grads_out = output_call(meta, kept, pairs, returned, slots)

    if direct:
        own_w, right_w, left_w, far_w, relay_w = weight_call(
            meta, saved, pairs, sums, (7, 13, 12, 14, 15), parts, half, rank
        )
        handed = along(relay_w, [(0, 1), (3, 2)])
        from_left = along(right_w, [(0, 1), (1, 2), (2, 3)])
        from_right = along(left_w, [(1, 0), (2, 1), (3, 2)])
        far_w = (far_w.astype(F32) + handed.astype(F32)).astype(BF16)
        from_far = along(far_w, [(0, 2), (1, 3), (2, 0), (3, 1)])
        messages = [own_w, from_left, from_right, from_far]
        down_sum, up_sum, gain_sum = total_call(messages, 1.0 / devices, half)
    else:
        (whole,) = weight_call(meta, saved, pairs, sums, (7,), parts, half, rank)
        down_sum, up_sum, gain_sum = total_call([whole], 1.0 / devices, half)
        scatter = functools.partial(lax.psum_scatter, axis_name="dp", scatter_dimension=1, tiled=True)
        down_sum, up_sum, gain_sum = scatter(down_sum), scatter(up_sum), scatter(gain_sum)
    return grads_out[None], down_sum[None], up_sum[None], gain_sum[None]


def solution(mesh):
    in_specs = (
        P(("groups", "dp"), None),
        P("groups"),
        P("groups"),
        P("section", None, "dp", None),
        P("section", None, "dp", None),
        P("section", None, None),
        P("dp", None),
        P(),
        P(),
    )
    out_specs = (
        P("section", ("groups", "dp"), None),
        P(("groups", "section"), None, "dp", None),
        P(("groups", "section"), None, "dp", None),
        P(("groups", "section"), None, "dp"),
    )
    return jax.shard_map(device_program, mesh=mesh, in_specs=in_specs, out_specs=out_specs, check_vma=False)
```

```python
import functools

import jax
import jax.numpy as jnp
from jax import lax
from jax.experimental import pallas as pl
from jax.experimental.pallas import tpu as pltpu
from jax.sharding import PartitionSpec as P


EPS = 1e-06
LOSS_SCALE = 4096.0
FIXED_POINT = 256.0
QUAD = 4
LONG = 3
F32 = jnp.float32
BF16 = jnp.bfloat16
ANY = pl.BlockSpec(memory_space=pl.ANY)
HBM = pl.BlockSpec(memory_space=pltpu.HBM)
VMEM = pl.BlockSpec(memory_space=pltpu.VMEM)


def dot(left, right):
    return jnp.dot(left, right, preferred_element_type=F32)


def dot_nt(left, right):
    return lax.dot_general(left, right, (((1,), (1,)), ((), ())), preferred_element_type=F32)


def dot_tn(left, right):
    return lax.dot_general(left, right, (((0,), (0,)), ((), ())), preferred_element_type=F32)


def norm_parts(rows):
    values = rows.astype(F32)
    inverse = lax.rsqrt(jnp.mean(values * values, axis=-1, keepdims=True) + EPS)
    return values * inverse, inverse


def head_logits(normed, gain_ref, scaled_ref, meta_ref, pieces):
    scaled_ref[...] = (normed * gain_ref[...].astype(F32)).astype(BF16)
    part = pieces[0].shape[0]
    total = None
    for k, piece in enumerate(pieces):
        start = pl.multiple_of(meta_ref[0, 8 + k] * part, part)
        term = dot(scaled_ref[:, pl.ds(start, part)], piece[...])
        total = term if total is None else total + term
    return total


def score_kernel(count, unit, meta_ref, kept_ref, teacher_ref, rows_ref, gain_ref, out_ref, *rest):
    pieces, (coef_ref, scaled_ref) = rest[:count], rest[count:]
    step = pl.program_id(0)
    kept = kept_ref[meta_ref[0, 5]]

    @pl.when(step == 0)
    def _():
        coef_ref[...] = jnp.zeros_like(coef_ref)

    @pl.when(jnp.logical_and(meta_ref[0, 4] == 1, step * unit < kept))
    def _():
        normed, _ = norm_parts(rows_ref[...])
        logits = head_logits(normed, gain_ref, scaled_ref, meta_ref, pieces)
        scores = jax.nn.silu(logits) * out_ref[...].astype(F32)
        place = lax.broadcasted_iota(jnp.int32, scores.shape, 0) + step * unit
        scores = jnp.where(place < kept, scores, 0.0)
        coef_ref[...] += jnp.broadcast_to(jnp.sum(scores), coef_ref.shape)

    @pl.when(step == pl.num_programs(0) - 1)
    def _():
        counts = jnp.full(coef_ref.shape, kept, jnp.int32).astype(F32)
        target = jnp.full(coef_ref.shape, teacher_ref[meta_ref[0, 5]], jnp.int32).astype(F32)
        score = coef_ref[...] / counts
        coef_ref[...] = 2.0 * LOSS_SCALE * (score - target / FIXED_POINT) / counts


def score_call(meta, kept, teacher, rows, gain, out, pieces, unit):
    slots, width = rows.shape
    keep = lambda *_: (0, 0)
    return pl.pallas_call(
        functools.partial(score_kernel, len(pieces), unit),
        grid_spec=pltpu.PrefetchScalarGridSpec(
            num_scalar_prefetch=3,
            grid=(slots // unit,),
            in_specs=[
                pl.BlockSpec((unit, width), lambda i, *_: (i, 0)),
                pl.BlockSpec(gain.shape, keep),
                pl.BlockSpec(out.shape, keep),
            ]
            + [pl.BlockSpec(p.shape, keep) for p in pieces],
            out_specs=pl.BlockSpec((8, 128), keep),
            scratch_shapes=[pltpu.VMEM((unit, width), BF16)],
        ),
        out_shape=jax.ShapeDtypeStruct((8, 128), F32),
        cost_estimate=pl.CostEstimate(
            flops=2 * slots * width * out.shape[1],
            transcendentals=slots * out.shape[1],
            bytes_accessed=12 * slots * width,
        ),
        compiler_params=pltpu.CompilerParams(vmem_limit_bytes=24 << 20),
        name="score",
    )(meta, kept, teacher, rows, gain, out, *pieces)


def head_kernel(count, meta_ref, dealt_ref, rows_ref, far_ref, own_ref, gain_ref, out_ref, *rest):
    pieces, (packet_ref, scaled_ref, normal_ref) = rest[:count], rest[count:]
    step = pl.program_id(0)

    @pl.when(meta_ref[0, 4] == 1)
    def _():
        rows = jnp.where(step == 0, dealt_ref[...], rows_ref[...])
        width = rows.shape[1]
        packet_ref[:, :width] = rows
        normed, inverse = norm_parts(rows)
        normal_ref[...] = normed
        logits = head_logits(normed, gain_ref, scaled_ref, meta_ref, pieces)
        coef = jnp.where(step == 0, far_ref[0:1, :], own_ref[0:1, :])
        sigma = jax.nn.sigmoid(logits)
        slope = sigma * (1.0 + logits * (1.0 - sigma))
        grad = (coef * out_ref[...].astype(F32) * slope).astype(BF16)
        part = pieces[0].shape[0]
        mean = jnp.zeros_like(inverse)
        spans = []
        for k, piece in enumerate(pieces):
            start = pl.multiple_of(meta_ref[0, 8 + k] * part, part)
            span = pl.ds(start, part)
            weighted = dot_nt(grad, piece[...]) * gain_ref[:, span].astype(F32)
            mean += jnp.sum(normal_ref[:, span] * weighted, axis=-1, keepdims=True)
            spans.append((span, weighted))
        mean = mean / normed.shape[1]
        for k, (span, weighted) in enumerate(spans):
            start = pl.multiple_of(meta_ref[0, 8 + k] * part + width, part)
            back = inverse * (weighted - normal_ref[:, span] * mean)
            packet_ref[:, pl.ds(start, part)] = back.astype(BF16)


def head_call(meta, dealt, rows, far, own, gain, out, pieces, total):
    block, width = dealt.shape
    keep = lambda *_: (0, 0)
    return pl.pallas_call(
        functools.partial(head_kernel, len(pieces)),
        grid_spec=pltpu.PrefetchScalarGridSpec(
            num_scalar_prefetch=1,
            grid=(total // block,),
            in_specs=[
                pl.BlockSpec((block, width), keep),
                pl.BlockSpec((block, width), lambda i, *_: (jnp.maximum(i - 1, 0), 0)),
                pl.BlockSpec((8, 128), keep),
                pl.BlockSpec((8, 128), keep),
                pl.BlockSpec(gain.shape, keep),
                pl.BlockSpec(out.shape, keep),
            ]
            + [pl.BlockSpec(p.shape, keep) for p in pieces],
            out_specs=pl.BlockSpec((block, 2 * width), lambda i, *_: (i, 0)),
            scratch_shapes=[pltpu.VMEM((block, width), BF16), pltpu.VMEM((block, width), F32)],
        ),
        out_shape=jax.ShapeDtypeStruct((total, 2 * width), BF16),
        cost_estimate=pl.CostEstimate(
            flops=4 * total * width * out.shape[1],
            transcendentals=total * out.shape[1],
            bytes_accessed=24 * total * width,
        ),
        compiler_params=pltpu.CompilerParams(vmem_limit_bytes=24 << 20),
        name="head",
    )(meta, dealt, rows, far, own, gain, out, *pieces)


def pack_kernel(deals, meta_ref, down_ref, up_ref, rows_ref, *refs):
    outs, (message_s, deal_s, sem) = refs[: 2 + deals], refs[2 + deals :]
    count, rank = outs[0].shape[0] // 2, outs[0].shape[2]
    copies = []

    def copy(source, goal):
        copies.append(pltpu.make_async_copy(source, goal, sem.at[len(copies)]))
        copies[-1].start()

    for number, field in enumerate((3, 6)):
        index = meta_ref[0, field]
        copy(down_ref.at[index], message_s.at[number, pl.ds(0, count)])
        for c in range(count):
            copy(up_ref.at[index, :, pl.ds(c * rank, rank)], message_s.at[number, count + c])
    for k in range(deals):
        rows = deal_s.shape[1]
        start = pl.multiple_of(meta_ref[0, 20 + k], rows)
        copy(rows_ref.at[pl.ds(start, rows)], deal_s.at[k])
    each = 1 + count
    for number in range(2):
        for one in copies[number * each : (number + 1) * each]:
            one.wait()
        copy(message_s.at[number], outs[number])
    for k in range(deals):
        copies[2 * each + k].wait()
        copy(deal_s.at[k], outs[2 + k])
    for one in copies[2 * each + deals :]:
        one.wait()


def pack_call(meta, down, up, rows, deals, chunk):
    part, half = up.shape[1:]
    rank = down.shape[2]
    count = half // rank
    message = jax.ShapeDtypeStruct((2 * count, part, rank), BF16)
    deal = jax.ShapeDtypeStruct((chunk, rows.shape[1]), BF16)
    return pl.pallas_call(
        functools.partial(pack_kernel, deals),
        grid_spec=pltpu.PrefetchScalarGridSpec(
            num_scalar_prefetch=1,
            grid=(1,),
            in_specs=[HBM] * 3,
            out_specs=[HBM] * (2 + deals),
            scratch_shapes=[
                pltpu.VMEM((2,) + message.shape, BF16),
                pltpu.VMEM((deals,) + deal.shape, BF16),
                pltpu.SemaphoreType.DMA((2 * (2 + count) + 2 * deals,)),
            ],
        ),
        out_shape=[message] * 2 + [deal] * deals,
        compiler_params=pltpu.CompilerParams(vmem_limit_bytes=60 << 20),
        name="pack",
    )(meta, down.reshape(2, count, part, rank), up, rows)


def assemble_kernel(plan, meta_ref, *refs):
    pieces, (down_ref, up_ref, sem) = refs[: len(plan)], refs[-3:]
    spans = up_ref.shape[1]

    def each(action):
        for number, (ref, (branch_field, place_field, valid_field)) in enumerate(zip(pieces, plan)):
            index, spot = meta_ref[0, branch_field], meta_ref[0, place_field]
            part = ref.shape[1]
            start = pl.multiple_of(spot * part, part)
            copies = [
                pltpu.make_async_copy(
                    ref.at[pl.ds(0, spans)],
                    down_ref.at[index, pl.ds(spot * spans, spans)],
                    sem.at[2 * number],
                ),
                pltpu.make_async_copy(
                    ref.at[pl.ds(spans, spans)],
                    up_ref.at[index, :, pl.ds(start, part)],
                    sem.at[2 * number + 1],
                ),
            ]

            @pl.when(meta_ref[0, valid_field] == 1)
            def _():
                for copy in copies:
                    action(copy)

    each(lambda copy: copy.start())
    each(lambda copy: copy.wait())


def assemble_call(meta, pieces, plan, half, held=()):
    rank = pieces[0].shape[2]
    part = pieces[0].shape[1]
    return pl.pallas_call(
        functools.partial(assemble_kernel, plan),
        grid_spec=pltpu.PrefetchScalarGridSpec(
            num_scalar_prefetch=1,
            grid=(1,),
            in_specs=[ANY] * len(pieces) + [VMEM] * len(held),
            out_specs=[VMEM] * 2,
            scratch_shapes=[pltpu.SemaphoreType.DMA((2 * len(pieces),))],
        ),
        out_shape=[
            jax.ShapeDtypeStruct((2, half // part, part, rank), BF16),
            jax.ShapeDtypeStruct((2, half // rank, rank, rank), BF16),
        ],
        input_output_aliases={1 + len(pieces) + i: i for i in range(len(held))},
        compiler_params=pltpu.CompilerParams(vmem_limit_bytes=8 << 20),
        name="assemble",
    )(meta, *pieces, *held)


def output_kernel(unit, plan, meta_ref, kept_ref, pairs_ref, *refs):
    pieces, (out_ref, zero_s, sem) = refs[: len(plan)], refs[len(plan) :]
    chunk = pieces[0].shape[0]
    own = pltpu.make_async_copy(
        pairs_ref.at[pl.ds(chunk, unit)], out_ref.at[pl.ds(0, unit)], sem.at[len(plan)]
    )
    own.start()
    long = kept_ref[meta_ref[0, 5]] > unit

    @pl.when(jnp.logical_not(long))
    def _():
        zero_s[...] = jnp.zeros_like(zero_s)
        copies = [
            pltpu.make_async_copy(
                zero_s, out_ref.at[pl.ds(unit + chunk * j, chunk)], sem.at[j]
            )
            for j in range(QUAD)
        ]
        for copy in copies:
            copy.start()
        for copy in copies:
            copy.wait()

    def each(action):
        for number, (piece, (place_field, valid_field)) in enumerate(zip(pieces, plan)):
            start = pl.multiple_of(unit + chunk * meta_ref[0, place_field], chunk)
            copy = pltpu.make_async_copy(piece, out_ref.at[pl.ds(start, chunk)], sem.at[number])

            @pl.when(jnp.logical_and(long, meta_ref[0, valid_field] == 1))
            def _():
                action(copy)

    each(lambda copy: copy.start())
    each(lambda copy: copy.wait())
    own.wait()


def output_call(meta, kept, pairs, pieces, plan, slots):
    chunk, width = pieces[0].shape
    return pl.pallas_call(
        functools.partial(output_kernel, slots // LONG, plan),
        grid_spec=pltpu.PrefetchScalarGridSpec(
            num_scalar_prefetch=2,
            grid=(1,),
            in_specs=[ANY] * (1 + len(pieces)),
            out_specs=ANY,
            scratch_shapes=[
                pltpu.VMEM((chunk, width), BF16),
                pltpu.SemaphoreType.DMA((len(plan) + 1,)),
            ],
        ),
        out_shape=jax.ShapeDtypeStruct((slots, width), BF16),
        compiler_params=pltpu.CompilerParams(vmem_limit_bytes=4 << 20),
        name="output",
    )(meta, kept, pairs, *pieces)


def stage_kernel(slot, held, firsts, kept_state, last, *refs):
    meta_ref, gain_ref, top_ref, down_s, up_s = refs[:5]
    arrived = dict(zip(held, refs[5 : 5 + len(held)]))
    rest = refs[5 + len(held) + kept_state :]
    if last:
        rest = rest[-1:] + rest[:-1]
    packet_ref, pairs_ref, saved_ref, sums_ref = rest[:4]
    first_ref = rest[4] if firsts else None
    packet_s, packet_sem = rest[4 + firsts :]
    rows, wide = packet_s.shape
    width = wide // 2
    half = width // 2
    spans, rank = up_s.shape[1], up_s.shape[2]
    per = down_s.shape[1] // spans
    source, micro = meta_ref[slot, 0], meta_ref[slot, 1]

    @pl.when(meta_ref[slot, 2] == 1)
    def _():
        place = pl.ds(pl.multiple_of(micro * rows, rows), rows)
        options = [
            (
                source == 0,
                [pltpu.make_async_copy(top_ref.at[place], packet_s, packet_sem.at[0])],
            )
        ]
        for kind, ref in arrived.items():
            copy = pltpu.make_async_copy(ref, packet_s, packet_sem.at[1 + kind])
            options.append((source == kind, [copy]))

        def each_option(action):
            for chosen, copies in options:

                @pl.when(chosen)
                def _():
                    for copy in copies:
                        action(copy)

        each_option(lambda copy: copy.start())
        each_option(lambda copy: copy.wait())

        def branch(index, values_ref, start, cot, base, less, goal, plus, result):
            def span(c):
                return slice(c * rank, (c + 1) * rank)

            def take(ref, origin, c):
                return ref[:, origin + c * rank : origin + (c + 1) * rank].astype(F32)

            total = None
            for c in range(spans):
                values = take(values_ref, start, c)
                term = jnp.sum(values * values, axis=-1, keepdims=True)
                total = term if total is None else total + term
            inverse = lax.rsqrt(total / half + EPS)
            for c in range(spans):
                gain = gain_ref[index : index + 1, span(c)].astype(F32)
                scaled = (take(values_ref, start, c) * inverse * gain).astype(BF16)
                saved_ref[place, base + c * rank : base + (c + 1) * rank] = scaled
            down = down_s[index].reshape(half, rank)
            pre = dot(saved_ref[place, base : base + half], down)
            sigma = jax.nn.sigmoid(pre)
            hidden = (pre * sigma).astype(BF16)
            saved_ref[place, base + half : base + half + rank] = hidden
            grad_hidden = None
            for c in range(spans):
                term = dot_nt(cot(c), up_s[index, c])
                grad_hidden = term if grad_hidden is None else grad_hidden + term
            slope = sigma * (1.0 + pre * (1.0 - sigma))
            grad_pre = (grad_hidden * slope).astype(BF16)
            saved_ref[place, base + half + rank : base + half + 2 * rank] = grad_pre
            mean = jnp.sum(grad_pre.astype(F32) * pre, axis=-1, keepdims=True) / half
            for c in range(spans):
                output = dot(hidden, up_s[index, c])
                packet_ref[:, goal + c * rank : goal + (c + 1) * rank] = (
                    take(packet_s, less, c) - output
                ).astype(BF16)
            for c in range(spans):
                part = down_s[index, c * per : (c + 1) * per].reshape(rank, rank)
                grad_scaled = dot_nt(grad_pre, part)
                normed = take(values_ref, start, c) * inverse
                sums_ref[micro, index : index + 1, span(c)] = jnp.sum(
                    grad_scaled * normed, axis=0, keepdims=True
                )
                gain = gain_ref[index : index + 1, span(c)].astype(F32)
                back = inverse * (grad_scaled * gain - normed * mean)
                value = (take(packet_s, plus, c) + back).astype(BF16)
                packet_ref[:, result + c * rank : result + (c + 1) * rank] = value
                low = result - width + c * rank
                pairs_ref[place, low : low + rank] = value

        block = half + 2 * rank
        saved_ref[place, 2 * block :] = packet_s[:, width + half :]
        branch(
            1,
            packet_s,
            0,
            lambda c: packet_s[:, width + half + c * rank : width + half + (c + 1) * rank],
            block,
            half,
            half,
            width,
            width,
        )
        branch(
            0,
            packet_ref,
            half,
            lambda c: packet_ref[:, width + c * rank : width + (c + 1) * rank],
            0,
            0,
            0,
            width + half,
            width + half,
        )
        if firsts:

            @pl.when(micro == 0)
            def _():
                first_ref[...] = packet_ref[:, width:]


def stage_call(slot, meta, gains, top, weights, arrived, state, shapes, chunk, last):
    _, wide = top.shape
    half, rank = wide // 4, weights[0].shape[3]
    rows = chunk
    held = tuple(arrived)
    n_in = 5 + len(held)
    packet = jax.ShapeDtypeStruct((rows, wide), BF16)
    outs = shapes if last else [packet] + shapes
    scratch = [pltpu.VMEM(packet.shape, BF16), pltpu.SemaphoreType.DMA((4,))]
    scratch += [pltpu.VMEM(packet.shape, BF16)] if last else []
    shift = len(outs) - len(shapes)
    outs = pl.pallas_call(
        functools.partial(stage_kernel, slot, held, len(shapes) - 3, len(state), last),
        grid_spec=pltpu.PrefetchScalarGridSpec(
            num_scalar_prefetch=1,
            grid=(1,),
            in_specs=[pl.BlockSpec(gains.shape, lambda *_: (0, 0)), ANY]
            + [VMEM] * (2 + len(held) + len(state)),
            out_specs=[VMEM] * len(outs),
            scratch_shapes=scratch,
        ),
        out_shape=outs,
        input_output_aliases={n_in + i: shift + i for i in range(len(state))},
        cost_estimate=pl.CostEstimate(
            flops=16 * 2 * rows * half * rank, transcendentals=0, bytes_accessed=4 * rows * wide
        ),
        compiler_params=pltpu.CompilerParams(vmem_limit_bytes=6 << 20),
        name="stage",
    )(meta, gains, top, *weights, *arrived.values(), *state)
    outs = list(outs)
    return (None, outs) if last else (outs[0], outs[1:])


def weight_kernel(fields, meta_ref, saved_ref, first_ref, sums_ref, *refs):
    outs = refs[: len(fields)]
    down_s, up_s, gain_s, sem = refs[len(fields) :]
    spans, rank = up_s.shape[1], up_s.shape[2]
    half = spans * rank
    part = outs[0].shape[1]
    parts = rank // part
    block = half + 2 * rank
    copies = []

    def send(source, goal):
        copies.append(pltpu.make_async_copy(source, goal, sem.at[len(copies)]))
        copies[-1].start()

    spots = [meta_ref[0, field] for field in fields]
    for index in (1, 0):
        base = block * index
        scaled = saved_ref[:, base : base + half]
        hidden = saved_ref[:, base + half : base + half + rank]
        grad_pre = saved_ref[:, base + half + rank : base + block]
        cot = saved_ref[:, 2 * block : 2 * block + half] if index == 1 else first_ref[:, :half]
        for c in range(spans):
            up_s[index, c] = dot_tn(hidden, cot[:, c * rank : (c + 1) * rank]).astype(BF16)
        for out, spot in zip(outs, spots):
            start = pl.multiple_of(spot * part, part)
            send(
                up_s.at[index, :, pl.ds(start, part)],
                out.at[pl.ds((2 * index + 1) * spans, spans)],
            )
        down_s[index] = dot_tn(scaled, grad_pre).astype(BF16).reshape(down_s.shape[1:])
        for out, spot in zip(outs, spots):
            send(
                down_s.at[index, pl.ds(spot * spans, spans)],
                out.at[pl.ds(2 * index * spans, spans)],
            )
    gain_s[...] = jnp.zeros_like(gain_s)
    for number, (out, spot) in enumerate(zip(outs, spots)):
        size = half // parts
        for row, low in enumerate(range(0, size, rank)):
            high = min(low + rank, size)
            start = pl.multiple_of(spot * size + low, 128)
            gain = jnp.sum(sums_ref[:, :, pl.ds(start, high - low)], axis=0)
            gain_s[number, 0, 8 * row : 8 * row + 8, 0 : high - low] = gain.astype(BF16)
        send(gain_s.at[number], out.at[pl.ds(4 * spans, 1)])
    for copy in copies:
        copy.wait()


def weight_call(meta, saved, pairs, sums, fields, parts, half, rank):
    spans, part = half // rank, rank // parts
    return pl.pallas_call(
        functools.partial(weight_kernel, fields),
        grid_spec=pltpu.PrefetchScalarGridSpec(
            num_scalar_prefetch=1,
            grid=(1,),
            in_specs=[VMEM] * 3,
            out_specs=[HBM] * len(fields),
            scratch_shapes=[
                pltpu.VMEM((2, parts * spans, part, rank), BF16),
                pltpu.VMEM((2, spans, rank, rank), BF16),
                pltpu.VMEM((len(fields), 1, part, rank), BF16),
                pltpu.SemaphoreType.DMA((5 * len(fields),)),
            ],
        ),
        out_shape=[jax.ShapeDtypeStruct((4 * spans + 1, part, rank), BF16)] * len(fields),
        compiler_params=pltpu.CompilerParams(vmem_limit_bytes=16 << 20),
        name="weight",
    )(meta, saved, pairs, sums)


def total_kernel(count, scale, *refs):
    messages, (down_ref, up_ref, gain_ref) = refs[:count], refs[count:]
    spans = up_ref.shape[2] // messages[0].shape[2]
    rank = messages[0].shape[2]

    def total(*where):
        out = messages[0][where].astype(F32)
        for message in messages[1:]:
            out += message[where].astype(F32)
        return out * scale

    for index in range(2):
        base = 2 * index * spans
        down_ref[index] = total(slice(base, base + spans))
        for c in range(spans):
            up_ref[index, :, c * rank : (c + 1) * rank] = total(base + spans + c)
    size = gain_ref.shape[1]
    for row, low in enumerate(range(0, size, rank)):
        high = min(low + rank, size)
        block = total(4 * spans)
        gain_ref[:, low:high] = block[8 * row : 8 * row + 2, 0 : high - low]


def total_call(messages, scale, half):
    _, part, rank = messages[0].shape
    spans = half // rank
    down, up, gain = pl.pallas_call(
        functools.partial(total_kernel, len(messages), scale),
        out_shape=[
            jax.ShapeDtypeStruct((2, spans, part, rank), F32),
            jax.ShapeDtypeStruct((2, part, half), F32),
            jax.ShapeDtypeStruct((2, spans * part), F32),
        ],
        compiler_params=pltpu.CompilerParams(vmem_limit_bytes=24 << 20),
        name="total",
    )(*messages)
    return down.reshape(2, spans * part, rank), up, gain


def device_program(top_pair, kept, teacher, down_proj, up_proj, gains, head_proj, head_gain, head_out):
    devices = lax.axis_size("dp")
    sections = lax.axis_size("section")
    own = lax.axis_index("dp")
    section = lax.axis_index("section")
    side = lax.axis_index("groups")
    slots, width = top_pair.shape
    half, rank = width // 2, down_proj.shape[3]
    unit = slots // LONG
    chunk = (LONG - 1) * unit // QUAD
    rows_total = unit + chunk
    micros = rows_total // chunk
    quads = devices // QUAD
    place = own % QUAD
    top = sections - 1
    via = 1 if sections == 4 else top
    direct = devices == QUAD and lax.axis_size("groups") == 2 and sections == 4
    parts = QUAD if direct else 1

    def shift_pairs(k, lane=None):
        out = []
        for q in range(quads):
            for i in range(QUAD):
                source, goal = QUAD * q + i, QUAD * q + (i + k) % QUAD
                if lane is not None:
                    source, goal = source * sections + lane, goal * sections + lane
                out.append((source, goal))
        return out

    ids = jnp.arange(devices, dtype=jnp.int32)
    is_longest = jnp.logical_and(ids // QUAD == own // QUAD, kept > unit)
    longest = jnp.sum(jnp.where(is_longest, ids % QUAD, 0))
    mine = 1 - side if direct else jnp.zeros((), jnp.int32)
    is_top = section == top

    offsets = {top: 0}
    for s in range(top, 0, -1):
        offsets[s - 1] = offsets[s] + (1 if s % 2 == 1 else 2)
    count = micros + offsets[0]
    behind = (top - section) + (top // 2 - section // 2)
    source = jnp.where(is_top, 0, jnp.where(section % 2 == 0, 1, 2))
    step = jnp.arange(count, dtype=jnp.int32) - behind
    last = parts - 1
    fields = [
        source,
        jnp.clip(step, 0, micros - 1),
        jnp.logical_and(step >= 0, step < micros),
        mine,
        is_top,
        own,
        1 - mine,
        own if direct else 0,
    ]
    fields += [(own - k) % parts for k in range(QUAD)]
    fields += [
        jnp.clip(own - 1, 0, last),
        jnp.clip(own + 1, 0, last),
        (own + 2) % parts,
        jnp.clip(last - own, 0, last),
        own >= 1,
        own <= 2,
        jnp.logical_or(own == 0, own == 3),
        1,
    ]
    fields += [unit + chunk * ((place + k) % QUAD) for k in range(1, QUAD)]
    fields += [(place - k) % QUAD for k in range(QUAD)]
    meta = jnp.stack(
        [jnp.broadcast_to(jnp.asarray(f).astype(jnp.int32), (count,)) for f in fields], axis=1
    )

    if direct:
        down, up = down_proj[0], up_proj[0]
    else:
        down = lax.all_gather(down_proj[0], "dp", axis=1, tiled=True)
        up = lax.all_gather(up_proj[0], "dp", axis=1, tiled=True)
    mine_msg, other_msg, *deals = pack_call(meta, down, up, top_pair, QUAD - 1, chunk)
    pieces, plan = [mine_msg, other_msg], [(3, 7, 19), (6, 7, 19)]

    dealt = lax.dynamic_slice_in_dim(top_pair, unit + chunk * place, chunk)
    for k, deal in enumerate(deals, 1):
        other = lax.ppermute(deal, ("dp", "section"), shift_pairs(k, via))
        dealt = jnp.where((place - k) % QUAD == longest, other, dealt)
    if direct:
        head_pieces = [head_proj]
        for k in range(1, QUAD):
            head_pieces.append(lax.ppermute(head_proj, ("dp", "section"), shift_pairs(k, top)))
        dealt = lax.ppermute(dealt, "section", [(via, top)])

        def along(array, pairs):
            return lax.ppermute(array, "dp", pairs)

        def across(array, valid):
            pairs = [(QUAD * g + i, QUAD * (1 - g) + i) for g in (0, 1) for i in valid]
            return lax.ppermute(array, ("groups", "dp"), pairs)

        right = along(mine_msg, [(0, 1), (1, 2), (2, 3)])
        left = along(mine_msg, [(1, 0), (2, 1), (3, 2)])
        far = along(mine_msg, [(0, 2), (1, 3), (2, 0), (3, 1)])
        relay = along(far, [(1, 0), (2, 3)])
        for piece, place_field, valid_field, valid in (
            (right, 12, 16, (1, 2, 3)),
            (left, 13, 17, (0, 1, 2)),
            (far, 14, 19, (0, 1, 2, 3)),
            (relay, 15, 18, (0, 3)),
        ):
            pieces += [piece, across(piece, valid)]
            plan += [(3, place_field, valid_field), (6, place_field, valid_field)]
    else:
        head_pieces = [lax.all_gather(head_proj, "dp", axis=0, tiled=True)]

    gain_row, out_row = head_gain[None], head_out[None]
    coef = score_call(meta, kept, teacher, top_pair, gain_row, out_row, head_pieces, unit)
    far_coef = coef
    for k in range(1, QUAD):
        other = lax.ppermute(coef, ("dp", "section"), shift_pairs(k, top))
        far_coef = jnp.where((place - k) % QUAD == longest, other, far_coef)
    packets = head_call(meta, dealt, top_pair, far_coef, coef, gain_row, out_row, head_pieces, rows_total)

    shapes = [
        jax.ShapeDtypeStruct((rows_total, width), BF16),
        jax.ShapeDtypeStruct((rows_total, 2 * (half + 2 * rank) + half), BF16),
        jax.ShapeDtypeStruct((micros, 8, half), F32),
        jax.ShapeDtypeStruct((chunk, width), BF16),
    ]
    state = []
    weights = assemble_call(meta, pieces[:8], plan[:8], half)
    if direct:
        weights = assemble_call(meta, pieces[8:], plan[8:], half, weights)
    near, far_in = {}, {}
    for slot in range(count):
        arrived = {1: near.get(slot - 1), 2: far_in.get(slot - 2)}
        arrived = {kind: array for kind, array in arrived.items() if array is not None}
        if slot > offsets[0]:
            shapes = shapes[:3]
        packet, state = stage_call(
            slot, meta, gains[0], packets, weights, arrived, state, shapes, chunk, slot == count - 1
        )
        live = [s for s in range(1, sections) if 0 <= slot - offsets[s] < micros]
        for table, odd in ((far_in, 0), (near, 1)):
            hops = [(s, s - 1) for s in live if s % 2 == odd]
            if hops:
                table[slot] = lax.ppermute(packet, "section", hops)
        if slot == offsets[0]:
            piece = state.pop()
    pairs, saved, sums = state

    returned, home_plan = [piece], [(23, 19)]
    if direct:
        far_home = along(piece, [(0, 2), (1, 3), (2, 0), (3, 1)])
        returned += [along(piece, [(0, 1), (1, 2), (2, 3)]), along(piece, [(1, 0), (2, 1), (3, 2)])]
        returned += [far_home, along(far_home, [(1, 0), (2, 3)])]
        home_plan += [(12, 16), (13, 17), (14, 19), (15, 18)]
    else:
        for k in range(1, QUAD):
            returned.append(lax.ppermute(piece, "dp", shift_pairs(k)))
            home_plan.append((23 + k, 19))
    grads_out = output_call(meta, kept, pairs, returned, home_plan, slots)

    if direct:
        own_w, right_w, left_w, far_w, relay_w = weight_call(
            meta, saved, pairs, sums, (7, 13, 12, 14, 15), parts, half, rank
        )
        handed = along(relay_w, [(0, 1), (3, 2)])
        outer = along(far_w, [(0, 2), (3, 1)])
        from_left = along(right_w, [(0, 1), (1, 2), (2, 3)])
        from_right = along(left_w, [(1, 0), (2, 1), (3, 2)])
        inner = along((far_w.astype(F32) + handed.astype(F32)).astype(BF16), [(1, 3), (2, 0)])
        messages = [own_w, from_left, from_right, outer, inner]
        down_sum, up_sum, gain_sum = total_call(messages, 1.0 / devices, half)
    else:
        (whole,) = weight_call(meta, saved, pairs, sums, (7,), parts, half, rank)
        down_sum, up_sum, gain_sum = total_call([whole], 1.0 / devices, half)
        scatter = functools.partial(lax.psum_scatter, axis_name="dp", scatter_dimension=1, tiled=True)
        down_sum, up_sum, gain_sum = scatter(down_sum), scatter(up_sum), scatter(gain_sum)
    return grads_out[None], down_sum[None], up_sum[None], gain_sum[None]


def solution(mesh):
    in_specs = (
        P(("groups", "dp"), None),
        P("groups"),
        P("groups"),
        P("section", None, "dp", None),
        P("section", None, "dp", None),
        P("section", None, None),
        P("dp", None),
        P(),
        P(),
    )
    out_specs = (
        P("section", ("groups", "dp"), None),
        P(("groups", "section"), None, "dp", None),
        P(("groups", "section"), None, "dp", None),
        P(("groups", "section"), None, "dp"),
    )
    return jax.shard_map(device_program, mesh=mesh, in_specs=in_specs, out_specs=out_specs, check_vma=False)
```

```python
import functools

import jax
import jax.numpy as jnp
from jax import lax
from jax.experimental import pallas as pl
from jax.experimental.pallas import tpu as pltpu
from jax.sharding import PartitionSpec as P


EPS = 1e-06
LOSS_SCALE = 4096.0
FIXED_POINT = 256.0
QUAD = 4
LONG = 3
F32 = jnp.float32
BF16 = jnp.bfloat16
ANY = pl.BlockSpec(memory_space=pl.ANY)
HBM = pl.BlockSpec(memory_space=pltpu.HBM)
VMEM = pl.BlockSpec(memory_space=pltpu.VMEM)


def dot(left, right):
    return jnp.dot(left, right, preferred_element_type=F32)


def dot_nt(left, right):
    return lax.dot_general(left, right, (((1,), (1,)), ((), ())), preferred_element_type=F32)


def dot_tn(left, right):
    return lax.dot_general(left, right, (((0,), (0,)), ((), ())), preferred_element_type=F32)


def norm_parts(rows):
    values = rows.astype(F32)
    inverse = lax.rsqrt(jnp.mean(values * values, axis=-1, keepdims=True) + EPS)
    return values * inverse, inverse


def head_logits(normed, gain_ref, scaled_ref, meta_ref, pieces):
    scaled_ref[...] = (normed * gain_ref[...].astype(F32)).astype(BF16)
    part = pieces[0].shape[0]
    total = None
    for k, piece in enumerate(pieces):
        start = pl.multiple_of(meta_ref[0, 8 + k] * part, part)
        term = dot(scaled_ref[:, pl.ds(start, part)], piece[...])
        total = term if total is None else total + term
    return total


def score_kernel(count, unit, meta_ref, kept_ref, teacher_ref, rows_ref, gain_ref, out_ref, *rest):
    pieces, (coef_ref, scaled_ref) = rest[:count], rest[count:]
    step = pl.program_id(0)
    kept = kept_ref[meta_ref[0, 5]]

    @pl.when(step == 0)
    def _():
        coef_ref[...] = jnp.zeros_like(coef_ref)

    @pl.when(jnp.logical_and(meta_ref[0, 4] == 1, step * unit < kept))
    def _():
        normed, _ = norm_parts(rows_ref[...])
        logits = head_logits(normed, gain_ref, scaled_ref, meta_ref, pieces)
        scores = jax.nn.silu(logits) * out_ref[...].astype(F32)
        place = lax.broadcasted_iota(jnp.int32, scores.shape, 0) + step * unit
        scores = jnp.where(place < kept, scores, 0.0)
        coef_ref[...] += jnp.broadcast_to(jnp.sum(scores), coef_ref.shape)

    @pl.when(step == pl.num_programs(0) - 1)
    def _():
        counts = jnp.full(coef_ref.shape, kept, jnp.int32).astype(F32)
        target = jnp.full(coef_ref.shape, teacher_ref[meta_ref[0, 5]], jnp.int32).astype(F32)
        score = coef_ref[...] / counts
        coef_ref[...] = 2.0 * LOSS_SCALE * (score - target / FIXED_POINT) / counts


def score_call(meta, kept, teacher, rows, gain, out, pieces, unit):
    slots, width = rows.shape
    keep = lambda *_: (0, 0)
    return pl.pallas_call(
        functools.partial(score_kernel, len(pieces), unit),
        grid_spec=pltpu.PrefetchScalarGridSpec(
            num_scalar_prefetch=3,
            grid=(slots // unit,),
            in_specs=[
                pl.BlockSpec((unit, width), lambda i, *_: (i, 0)),
                pl.BlockSpec(gain.shape, keep),
                pl.BlockSpec(out.shape, keep),
            ]
            + [pl.BlockSpec(p.shape, keep) for p in pieces],
            out_specs=pl.BlockSpec((8, 128), keep),
            scratch_shapes=[pltpu.VMEM((unit, width), BF16)],
        ),
        out_shape=jax.ShapeDtypeStruct((8, 128), F32),
        cost_estimate=pl.CostEstimate(
            flops=2 * slots * width * out.shape[1],
            transcendentals=slots * out.shape[1],
            bytes_accessed=12 * slots * width,
        ),
        compiler_params=pltpu.CompilerParams(vmem_limit_bytes=24 << 20),
        name="score",
    )(meta, kept, teacher, rows, gain, out, *pieces)


def head_kernel(count, meta_ref, dealt_ref, rows_ref, far_ref, own_ref, gain_ref, out_ref, *rest):
    pieces, (packet_ref, scaled_ref, normal_ref) = rest[:count], rest[count:]
    step = pl.program_id(0)

    @pl.when(meta_ref[0, 4] == 1)
    def _():
        rows = jnp.where(step == 0, dealt_ref[...], rows_ref[...])
        width = rows.shape[1]
        packet_ref[:, :width] = rows
        normed, inverse = norm_parts(rows)
        normal_ref[...] = normed
        logits = head_logits(normed, gain_ref, scaled_ref, meta_ref, pieces)
        coef = jnp.where(step == 0, far_ref[0:1, :], own_ref[0:1, :])
        sigma = jax.nn.sigmoid(logits)
        slope = sigma * (1.0 + logits * (1.0 - sigma))
        grad = (coef * out_ref[...].astype(F32) * slope).astype(BF16)
        part = pieces[0].shape[0]
        mean = jnp.zeros_like(inverse)
        spans = []
        for k, piece in enumerate(pieces):
            start = pl.multiple_of(meta_ref[0, 8 + k] * part, part)
            span = pl.ds(start, part)
            weighted = dot_nt(grad, piece[...]) * gain_ref[:, span].astype(F32)
            mean += jnp.sum(normal_ref[:, span] * weighted, axis=-1, keepdims=True)
            spans.append((span, weighted))
        mean = mean / normed.shape[1]
        for k, (span, weighted) in enumerate(spans):
            start = pl.multiple_of(meta_ref[0, 8 + k] * part + width, part)
            back = inverse * (weighted - normal_ref[:, span] * mean)
            packet_ref[:, pl.ds(start, part)] = back.astype(BF16)


def head_call(meta, dealt, rows, far, own, gain, out, pieces, total):
    block, width = dealt.shape
    keep = lambda *_: (0, 0)
    return pl.pallas_call(
        functools.partial(head_kernel, len(pieces)),
        grid_spec=pltpu.PrefetchScalarGridSpec(
            num_scalar_prefetch=1,
            grid=(total // block,),
            in_specs=[
                pl.BlockSpec((block, width), keep),
                pl.BlockSpec((block, width), lambda i, *_: (jnp.maximum(i - 1, 0), 0)),
                pl.BlockSpec((8, 128), keep),
                pl.BlockSpec((8, 128), keep),
                pl.BlockSpec(gain.shape, keep),
                pl.BlockSpec(out.shape, keep),
            ]
            + [pl.BlockSpec(p.shape, keep) for p in pieces],
            out_specs=pl.BlockSpec((block, 2 * width), lambda i, *_: (i, 0)),
            scratch_shapes=[pltpu.VMEM((block, width), BF16), pltpu.VMEM((block, width), F32)],
        ),
        out_shape=jax.ShapeDtypeStruct((total, 2 * width), BF16),
        cost_estimate=pl.CostEstimate(
            flops=4 * total * width * out.shape[1],
            transcendentals=total * out.shape[1],
            bytes_accessed=24 * total * width,
        ),
        compiler_params=pltpu.CompilerParams(vmem_limit_bytes=24 << 20),
        name="head",
    )(meta, dealt, rows, far, own, gain, out, *pieces)


def pack_kernel(deals, meta_ref, down_ref, up_ref, rows_ref, *refs):
    outs, (message_s, deal_s, sem) = refs[: 2 + deals], refs[2 + deals :]
    count, rank = outs[0].shape[0] // 2, outs[0].shape[2]
    copies = []

    def copy(source, goal):
        copies.append(pltpu.make_async_copy(source, goal, sem.at[len(copies)]))
        copies[-1].start()

    for number, field in enumerate((3, 6)):
        index = meta_ref[0, field]
        copy(down_ref.at[index], message_s.at[number, pl.ds(0, count)])
        for c in range(count):
            copy(up_ref.at[index, :, pl.ds(c * rank, rank)], message_s.at[number, count + c])
    for k in range(deals):
        rows = deal_s.shape[1]
        start = pl.multiple_of(meta_ref[0, 20 + k], rows)
        copy(rows_ref.at[pl.ds(start, rows)], deal_s.at[k])
    each = 1 + count
    for number in range(2):
        for one in copies[number * each : (number + 1) * each]:
            one.wait()
        copy(message_s.at[number], outs[number])
    for k in range(deals):
        copies[2 * each + k].wait()
        copy(deal_s.at[k], outs[2 + k])
    for one in copies[2 * each + deals :]:
        one.wait()


def pack_call(meta, down, up, rows, deals, chunk):
    part, half = up.shape[1:]
    rank = down.shape[2]
    count = half // rank
    message = jax.ShapeDtypeStruct((2 * count, part, rank), BF16)
    deal = jax.ShapeDtypeStruct((chunk, rows.shape[1]), BF16)
    return pl.pallas_call(
        functools.partial(pack_kernel, deals),
        grid_spec=pltpu.PrefetchScalarGridSpec(
            num_scalar_prefetch=1,
            grid=(1,),
            in_specs=[HBM] * 3,
            out_specs=[HBM] * (2 + deals),
            scratch_shapes=[
                pltpu.VMEM((2,) + message.shape, BF16),
                pltpu.VMEM((deals,) + deal.shape, BF16),
                pltpu.SemaphoreType.DMA((2 * (2 + count) + 2 * deals,)),
            ],
        ),
        out_shape=[message] * 2 + [deal] * deals,
        compiler_params=pltpu.CompilerParams(vmem_limit_bytes=60 << 20),
        name="pack",
    )(meta, down.reshape(2, count, part, rank), up, rows)


def assemble_kernel(plan, meta_ref, *refs):
    pieces, (down_ref, up_ref, sem) = refs[: len(plan)], refs[-3:]
    spans = up_ref.shape[1]

    def each(action):
        for number, (ref, (branch_field, place_field, valid_field)) in enumerate(zip(pieces, plan)):
            index, spot = meta_ref[0, branch_field], meta_ref[0, place_field]
            part = ref.shape[1]
            start = pl.multiple_of(spot * part, part)
            copies = [
                pltpu.make_async_copy(
                    ref.at[pl.ds(0, spans)],
                    down_ref.at[index, pl.ds(spot * spans, spans)],
                    sem.at[2 * number],
                ),
                pltpu.make_async_copy(
                    ref.at[pl.ds(spans, spans)],
                    up_ref.at[index, :, pl.ds(start, part)],
                    sem.at[2 * number + 1],
                ),
            ]

            @pl.when(meta_ref[0, valid_field] == 1)
            def _():
                for copy in copies:
                    action(copy)

    each(lambda copy: copy.start())
    each(lambda copy: copy.wait())


def assemble_call(meta, pieces, plan, half, held=()):
    rank = pieces[0].shape[2]
    part = pieces[0].shape[1]
    return pl.pallas_call(
        functools.partial(assemble_kernel, plan),
        grid_spec=pltpu.PrefetchScalarGridSpec(
            num_scalar_prefetch=1,
            grid=(1,),
            in_specs=[ANY] * len(pieces) + [VMEM] * len(held),
            out_specs=[VMEM] * 2,
            scratch_shapes=[pltpu.SemaphoreType.DMA((2 * len(pieces),))],
        ),
        out_shape=[
            jax.ShapeDtypeStruct((2, half // part, part, rank), BF16),
            jax.ShapeDtypeStruct((2, half // rank, rank, rank), BF16),
        ],
        input_output_aliases={1 + len(pieces) + i: i for i in range(len(held))},
        compiler_params=pltpu.CompilerParams(vmem_limit_bytes=8 << 20),
        name="assemble",
    )(meta, *pieces, *held)


def output_kernel(unit, plan, meta_ref, kept_ref, pairs_ref, *refs):
    pieces, (out_ref, zero_s, sem) = refs[: len(plan)], refs[len(plan) :]
    chunk = pieces[0].shape[0]
    own = pltpu.make_async_copy(
        pairs_ref.at[pl.ds(chunk, unit)], out_ref.at[pl.ds(0, unit)], sem.at[len(plan)]
    )
    own.start()
    long = kept_ref[meta_ref[0, 5]] > unit

    @pl.when(jnp.logical_not(long))
    def _():
        zero_s[...] = jnp.zeros_like(zero_s)
        copies = [
            pltpu.make_async_copy(
                zero_s, out_ref.at[pl.ds(unit + chunk * j, chunk)], sem.at[j]
            )
            for j in range(QUAD)
        ]
        for copy in copies:
            copy.start()
        for copy in copies:
            copy.wait()

    def each(action):
        for number, (piece, (place_field, valid_field)) in enumerate(zip(pieces, plan)):
            start = pl.multiple_of(unit + chunk * meta_ref[0, place_field], chunk)
            copy = pltpu.make_async_copy(piece, out_ref.at[pl.ds(start, chunk)], sem.at[number])

            @pl.when(jnp.logical_and(long, meta_ref[0, valid_field] == 1))
            def _():
                action(copy)

    each(lambda copy: copy.start())
    each(lambda copy: copy.wait())
    own.wait()


def output_call(meta, kept, pairs, pieces, plan, slots):
    chunk, width = pieces[0].shape
    return pl.pallas_call(
        functools.partial(output_kernel, slots // LONG, plan),
        grid_spec=pltpu.PrefetchScalarGridSpec(
            num_scalar_prefetch=2,
            grid=(1,),
            in_specs=[ANY] * (1 + len(pieces)),
            out_specs=ANY,
            scratch_shapes=[
                pltpu.VMEM((chunk, width), BF16),
                pltpu.SemaphoreType.DMA((len(plan) + 1,)),
            ],
        ),
        out_shape=jax.ShapeDtypeStruct((slots, width), BF16),
        compiler_params=pltpu.CompilerParams(vmem_limit_bytes=4 << 20),
        name="output",
    )(meta, kept, pairs, *pieces)


def stage_kernel(slot, held, firsts, kept_state, last, *refs):
    meta_ref, gain_ref, top_ref, down_s, up_s = refs[:5]
    arrived = dict(zip(held, refs[5 : 5 + len(held)]))
    rest = refs[5 + len(held) + kept_state :]
    if last:
        rest = rest[-1:] + rest[:-1]
    packet_ref, pairs_ref, saved_ref, sums_ref = rest[:4]
    first_ref = rest[4] if firsts else None
    packet_s, packet_sem = rest[4 + firsts :]
    rows, wide = packet_s.shape
    width = wide // 2
    half = width // 2
    spans, rank = up_s.shape[1], up_s.shape[2]
    per = down_s.shape[1] // spans
    source, micro = meta_ref[slot, 0], meta_ref[slot, 1]

    @pl.when(meta_ref[slot, 2] == 1)
    def _():
        place = pl.ds(pl.multiple_of(micro * rows, rows), rows)
        options = [
            (
                source == 0,
                [pltpu.make_async_copy(top_ref.at[place], packet_s, packet_sem.at[0])],
            )
        ]
        for kind, ref in arrived.items():
            copy = pltpu.make_async_copy(ref, packet_s, packet_sem.at[1 + kind])
            options.append((source == kind, [copy]))

        def each_option(action):
            for chosen, copies in options:

                @pl.when(chosen)
                def _():
                    for copy in copies:
                        action(copy)

        each_option(lambda copy: copy.start())
        each_option(lambda copy: copy.wait())

        def branch(index, values_ref, start, cot, base, less, goal, plus, result):
            def span(c):
                return slice(c * rank, (c + 1) * rank)

            def take(ref, origin, c):
                return ref[:, origin + c * rank : origin + (c + 1) * rank].astype(F32)

            total = None
            for c in range(spans):
                values = take(values_ref, start, c)
                term = jnp.sum(values * values, axis=-1, keepdims=True)
                total = term if total is None else total + term
            inverse = lax.rsqrt(total / half + EPS)
            for c in range(spans):
                gain = gain_ref[index : index + 1, span(c)].astype(F32)
                scaled = (take(values_ref, start, c) * inverse * gain).astype(BF16)
                saved_ref[place, base + c * rank : base + (c + 1) * rank] = scaled
            down = down_s[index].reshape(half, rank)
            pre = dot(saved_ref[place, base : base + half], down)
            sigma = jax.nn.sigmoid(pre)
            hidden = (pre * sigma).astype(BF16)
            saved_ref[place, base + half : base + half + rank] = hidden
            grad_hidden = None
            for c in range(spans):
                term = dot_nt(cot(c), up_s[index, c])
                grad_hidden = term if grad_hidden is None else grad_hidden + term
            slope = sigma * (1.0 + pre * (1.0 - sigma))
            grad_pre = (grad_hidden * slope).astype(BF16)
            saved_ref[place, base + half + rank : base + half + 2 * rank] = grad_pre
            mean = jnp.sum(grad_pre.astype(F32) * pre, axis=-1, keepdims=True) / half
            for c in range(spans):
                output = dot(hidden, up_s[index, c])
                packet_ref[:, goal + c * rank : goal + (c + 1) * rank] = (
                    take(packet_s, less, c) - output
                ).astype(BF16)
            for c in range(spans):
                part = down_s[index, c * per : (c + 1) * per].reshape(rank, rank)
                grad_scaled = dot_nt(grad_pre, part)
                normed = take(values_ref, start, c) * inverse
                sums_ref[micro, index : index + 1, span(c)] = jnp.sum(
                    grad_scaled * normed, axis=0, keepdims=True
                )
                gain = gain_ref[index : index + 1, span(c)].astype(F32)
                back = inverse * (grad_scaled * gain - normed * mean)
                value = (take(packet_s, plus, c) + back).astype(BF16)
                packet_ref[:, result + c * rank : result + (c + 1) * rank] = value
                low = result - width + c * rank
                pairs_ref[place, low : low + rank] = value

        block = half + 2 * rank
        saved_ref[place, 2 * block :] = packet_s[:, width + half :]
        branch(
            1,
            packet_s,
            0,
            lambda c: packet_s[:, width + half + c * rank : width + half + (c + 1) * rank],
            block,
            half,
            half,
            width,
            width,
        )
        branch(
            0,
            packet_ref,
            half,
            lambda c: packet_ref[:, width + c * rank : width + (c + 1) * rank],
            0,
            0,
            0,
            width + half,
            width + half,
        )
        if firsts:

            @pl.when(micro == 0)
            def _():
                first_ref[...] = packet_ref[:, width:]


def stage_call(slot, meta, gains, top, weights, arrived, state, shapes, chunk, last):
    _, wide = top.shape
    half, rank = wide // 4, weights[0].shape[3]
    rows = chunk
    held = tuple(arrived)
    n_in = 5 + len(held)
    packet = jax.ShapeDtypeStruct((rows, wide), BF16)
    outs = shapes if last else [packet] + shapes
    scratch = [pltpu.VMEM(packet.shape, BF16), pltpu.SemaphoreType.DMA((4,))]
    scratch += [pltpu.VMEM(packet.shape, BF16)] if last else []
    shift = len(outs) - len(shapes)
    outs = pl.pallas_call(
        functools.partial(stage_kernel, slot, held, len(shapes) - 3, len(state), last),
        grid_spec=pltpu.PrefetchScalarGridSpec(
            num_scalar_prefetch=1,
            grid=(1,),
            in_specs=[pl.BlockSpec(gains.shape, lambda *_: (0, 0)), ANY]
            + [VMEM] * (2 + len(held) + len(state)),
            out_specs=[VMEM] * len(outs),
            scratch_shapes=scratch,
        ),
        out_shape=outs,
        input_output_aliases={n_in + i: shift + i for i in range(len(state))},
        cost_estimate=pl.CostEstimate(
            flops=16 * 2 * rows * half * rank, transcendentals=0, bytes_accessed=4 * rows * wide
        ),
        compiler_params=pltpu.CompilerParams(vmem_limit_bytes=6 << 20),
        name="stage",
    )(meta, gains, top, *weights, *arrived.values(), *state)
    outs = list(outs)
    return (None, outs) if last else (outs[0], outs[1:])


def weight_kernel(fields, meta_ref, saved_ref, first_ref, sums_ref, *refs):
    outs = refs[: len(fields)]
    down_s, up_s, gain_s, sem = refs[len(fields) :]
    spans, rank = up_s.shape[1], up_s.shape[2]
    half = spans * rank
    part = outs[0].shape[1]
    parts = rank // part
    block = half + 2 * rank
    copies = []

    def send(number, source, goal):
        copies.append((number, pltpu.make_async_copy(source, goal, sem.at[len(copies)])))

        @pl.when(wanted[number])
        def _():
            copies[-1][1].start()

    spots = [meta_ref[0, place] for place, _ in fields]
    wanted = [meta_ref[0, valid] == 1 for _, valid in fields]
    gain_s[...] = jnp.zeros_like(gain_s)
    for number, (out, spot) in enumerate(zip(outs, spots)):
        size = half // parts
        for row, low in enumerate(range(0, size, rank)):
            high = min(low + rank, size)
            start = pl.multiple_of(spot * size + low, 128)
            gain = jnp.sum(sums_ref[:, :, pl.ds(start, high - low)], axis=0)
            gain_s[number, 0, 8 * row : 8 * row + 8, 0 : high - low] = gain.astype(BF16)
        send(number, gain_s.at[number], out.at[pl.ds(4 * spans, 1)])
    for index in (1, 0):
        base = block * index
        scaled = saved_ref[:, base : base + half]
        hidden = saved_ref[:, base + half : base + half + rank]
        grad_pre = saved_ref[:, base + half + rank : base + block]
        cot = saved_ref[:, 2 * block : 2 * block + half] if index == 1 else first_ref[:, :half]
        for c in range(spans):
            up_s[index, c] = dot_tn(hidden, cot[:, c * rank : (c + 1) * rank]).astype(BF16)
        for number, (out, spot) in enumerate(zip(outs, spots)):
            start = pl.multiple_of(spot * part, part)
            send(
                number,
                up_s.at[index, :, pl.ds(start, part)],
                out.at[pl.ds((2 * index + 1) * spans, spans)],
            )
        turned = dot_tn(grad_pre, scaled).astype(BF16)
        size = half // parts
        each, rest = rank // part, size % rank
        for p in range(parts):
            first, entry = p * size, p * spans
            for low in range(first, first + size - rest, rank):
                square = turned[:, low : low + rank].reshape(each, part, rank)
                down_s[index, entry : entry + each] = square
                entry += each
            for group in range(rank // rest if rest else 0):
                low = first + size - rest
                piece = turned[group * rest : (group + 1) * rest, low : low + rest]
                down_s[
                    index, entry : entry + rest // part, :, group * rest : (group + 1) * rest
                ] = piece.reshape(rest // part, part, rest)
        for number, (out, spot) in enumerate(zip(outs, spots)):
            send(
                number,
                down_s.at[index, pl.ds(spot * spans, spans)],
                out.at[pl.ds(2 * index * spans, spans)],
            )
    for number, copy in copies:

        @pl.when(wanted[number])
        def _():
            copy.wait()


def weight_call(meta, saved, pairs, sums, fields, parts, half, rank):
    spans, part = half // rank, rank // parts
    return pl.pallas_call(
        functools.partial(weight_kernel, fields),
        grid_spec=pltpu.PrefetchScalarGridSpec(
            num_scalar_prefetch=1,
            grid=(1,),
            in_specs=[VMEM] * 3,
            out_specs=[HBM] * len(fields),
            scratch_shapes=[
                pltpu.VMEM((2, parts * spans, part, rank), BF16),
                pltpu.VMEM((2, spans, rank, rank), BF16),
                pltpu.VMEM((len(fields), 1, part, rank), BF16),
                pltpu.SemaphoreType.DMA((5 * len(fields),)),
            ],
        ),
        out_shape=[jax.ShapeDtypeStruct((4 * spans + 1, part, rank), BF16)] * len(fields),
        compiler_params=pltpu.CompilerParams(vmem_limit_bytes=16 << 20),
        name="weight",
    )(meta, saved, pairs, sums)


def total_kernel(count, scale, *refs):
    messages, (down_ref, up_ref, gain_ref) = refs[:count], refs[count:]
    spans = up_ref.shape[2] // messages[0].shape[2]
    rank = messages[0].shape[2]

    def total(*where):
        out = messages[0][where].astype(F32)
        for message in messages[1:]:
            out += message[where].astype(F32)
        return out * scale

    for index in range(2):
        base = 2 * index * spans
        part = messages[0].shape[1]
        size = spans * part
        each, rest = rank // part, size % rank
        for entry in range(0, (size - rest) // part, each):
            square = total(slice(base + entry, base + entry + each)).reshape(rank, rank)
            down_ref[index, entry : entry + each] = square.T.reshape(each, part, rank)
        if rest:
            entry = (size - rest) // part
            block = total(slice(base + entry, base + spans)).reshape(rest, rank)
            for low in range(0, rank, rest):
                turned = block[:, low : low + rest].T.reshape(rest // part, part, rest)
                down_ref[index, entry:, :, low : low + rest] = turned
        for c in range(spans):
            up_ref[index, :, c * rank : (c + 1) * rank] = total(base + spans + c)
    size = gain_ref.shape[1]
    for row, low in enumerate(range(0, size, rank)):
        high = min(low + rank, size)
        block = total(4 * spans)
        gain_ref[:, low:high] = block[8 * row : 8 * row + 2, 0 : high - low]


def total_call(messages, scale, half):
    _, part, rank = messages[0].shape
    spans = half // rank
    down, up, gain = pl.pallas_call(
        functools.partial(total_kernel, len(messages), scale),
        out_shape=[
            jax.ShapeDtypeStruct((2, spans, part, rank), F32),
            jax.ShapeDtypeStruct((2, part, half), F32),
            jax.ShapeDtypeStruct((2, spans * part), F32),
        ],
        compiler_params=pltpu.CompilerParams(vmem_limit_bytes=24 << 20),
        name="total",
    )(*messages)
    return down.reshape(2, spans * part, rank), up, gain


def device_program(top_pair, kept, teacher, down_proj, up_proj, gains, head_proj, head_gain, head_out):
    devices = lax.axis_size("dp")
    sections = lax.axis_size("section")
    own = lax.axis_index("dp")
    section = lax.axis_index("section")
    side = lax.axis_index("groups")
    slots, width = top_pair.shape
    half, rank = width // 2, down_proj.shape[3]
    unit = slots // LONG
    chunk = (LONG - 1) * unit // QUAD
    rows_total = unit + chunk
    micros = rows_total // chunk
    quads = devices // QUAD
    place = own % QUAD
    top = sections - 1
    via = 1 if sections == 4 else top
    direct = devices == QUAD and lax.axis_size("groups") == 2 and sections == 4
    parts = QUAD if direct else 1

    def shift_pairs(k, lane=None):
        out = []
        for q in range(quads):
            for i in range(QUAD):
                source, goal = QUAD * q + i, QUAD * q + (i + k) % QUAD
                if lane is not None:
                    source, goal = source * sections + lane, goal * sections + lane
                out.append((source, goal))
        return out

    ids = jnp.arange(devices, dtype=jnp.int32)
    is_longest = jnp.logical_and(ids // QUAD == own // QUAD, kept > unit)
    longest = jnp.sum(jnp.where(is_longest, ids % QUAD, 0))
    mine = 1 - side if direct else jnp.zeros((), jnp.int32)
    is_top = section == top

    offsets = {top: 0}
    for s in range(top, 0, -1):
        offsets[s - 1] = offsets[s] + (1 if s % 2 == 1 else 2)
    count = micros + offsets[0]
    behind = (top - section) + (top // 2 - section // 2)
    source = jnp.where(is_top, 0, jnp.where(section % 2 == 0, 1, 2))
    step = jnp.arange(count, dtype=jnp.int32) - behind
    last = parts - 1
    fields = [
        source,
        jnp.clip(step, 0, micros - 1),
        jnp.logical_and(step >= 0, step < micros),
        mine,
        is_top,
        own,
        1 - mine,
        own if direct else 0,
    ]
    fields += [(own - k) % parts for k in range(QUAD)]
    fields += [
        jnp.clip(own - 1, 0, last),
        jnp.clip(own + 1, 0, last),
        (own + 2) % parts,
        jnp.clip(last - own, 0, last),
        own >= 1,
        own <= 2,
        jnp.logical_or(own == 0, own == 3),
        1,
    ]
    fields += [unit + chunk * ((place + k) % QUAD) for k in range(1, QUAD)]
    fields += [(place - k) % QUAD for k in range(QUAD)]
    meta = jnp.stack(
        [jnp.broadcast_to(jnp.asarray(f).astype(jnp.int32), (count,)) for f in fields], axis=1
    )

    if direct:
        down, up = down_proj[0], up_proj[0]
    else:
        down = lax.all_gather(down_proj[0], "dp", axis=1, tiled=True)
        up = lax.all_gather(up_proj[0], "dp", axis=1, tiled=True)
    mine_msg, other_msg, *deals = pack_call(meta, down, up, top_pair, QUAD - 1, chunk)
    pieces, plan = [mine_msg, other_msg], [(3, 7, 19), (6, 7, 19)]

    dealt = lax.dynamic_slice_in_dim(top_pair, unit + chunk * place, chunk)
    for k, deal in enumerate(deals, 1):
        other = lax.ppermute(deal, ("dp", "section"), shift_pairs(k, via))
        dealt = jnp.where((place - k) % QUAD == longest, other, dealt)
    if direct:
        head_pieces = [head_proj]
        for k in range(1, QUAD):
            head_pieces.append(lax.ppermute(head_proj, ("dp", "section"), shift_pairs(k, top)))
        dealt = lax.ppermute(dealt, "section", [(via, top)])

        def along(array, pairs):
            return lax.ppermute(array, "dp", pairs)

        def across(array, valid):
            pairs = [(QUAD * g + i, QUAD * (1 - g) + i) for g in (0, 1) for i in valid]
            return lax.ppermute(array, ("groups", "dp"), pairs)

        right = along(mine_msg, [(0, 1), (1, 2), (2, 3)])
        left = along(mine_msg, [(1, 0), (2, 1), (3, 2)])
        far = along(mine_msg, [(0, 2), (1, 3), (2, 0), (3, 1)])
        relay = along(far, [(1, 0), (2, 3)])
        for piece, place_field, valid_field, valid in (
            (right, 12, 16, (1, 2, 3)),
            (left, 13, 17, (0, 1, 2)),
            (far, 14, 19, (0, 1, 2, 3)),
            (relay, 15, 18, (0, 3)),
        ):
            pieces += [piece, across(piece, valid)]
            plan += [(3, place_field, valid_field), (6, place_field, valid_field)]
    else:
        head_pieces = [lax.all_gather(head_proj, "dp", axis=0, tiled=True)]

    gain_row, out_row = head_gain[None], head_out[None]
    coef = score_call(meta, kept, teacher, top_pair, gain_row, out_row, head_pieces, unit)
    far_coef = coef
    for k in range(1, QUAD):
        other = lax.ppermute(coef, ("dp", "section"), shift_pairs(k, top))
        far_coef = jnp.where((place - k) % QUAD == longest, other, far_coef)
    packets = head_call(meta, dealt, top_pair, far_coef, coef, gain_row, out_row, head_pieces, rows_total)

    shapes = [
        jax.ShapeDtypeStruct((rows_total, width), BF16),
        jax.ShapeDtypeStruct((rows_total, 2 * (half + 2 * rank) + half), BF16),
        jax.ShapeDtypeStruct((micros, 8, half), F32),
        jax.ShapeDtypeStruct((chunk, width), BF16),
    ]
    state = []
    weights = assemble_call(meta, pieces[:8], plan[:8], half)
    if direct:
        weights = assemble_call(meta, pieces[8:], plan[8:], half, weights)
    near, far_in = {}, {}
    for slot in range(count):
        arrived = {1: near.get(slot - 1), 2: far_in.get(slot - 2)}
        arrived = {kind: array for kind, array in arrived.items() if array is not None}
        if slot > offsets[0]:
            shapes = shapes[:3]
        packet, state = stage_call(
            slot, meta, gains[0], packets, weights, arrived, state, shapes, chunk, slot == count - 1
        )
        live = [s for s in range(1, sections) if 0 <= slot - offsets[s] < micros]
        for table, odd in ((far_in, 0), (near, 1)):
            hops = [(s, s - 1) for s in live if s % 2 == odd]
            if hops:
                table[slot] = lax.ppermute(packet, "section", hops)
        if slot == offsets[0]:
            piece = state.pop()
    pairs, saved, sums = state

    returned, home_plan = [piece], [(23, 19)]
    if direct:
        far_home = along(piece, [(0, 2), (1, 3), (2, 0), (3, 1)])
        returned += [along(piece, [(0, 1), (1, 2), (2, 3)]), along(piece, [(1, 0), (2, 1), (3, 2)])]
        returned += [far_home, along(far_home, [(1, 0), (2, 3)])]
        home_plan += [(12, 16), (13, 17), (14, 19), (15, 18)]
    else:
        for k in range(1, QUAD):
            returned.append(lax.ppermute(piece, "dp", shift_pairs(k)))
            home_plan.append((23 + k, 19))
    grads_out = output_call(meta, kept, pairs, returned, home_plan, slots)

    if direct:
        own_w, right_w, left_w, far_w, relay_w = weight_call(
            meta, saved, pairs, sums, ((7, 19), (13, 17), (12, 16), (14, 19), (15, 18)), parts, half, rank
        )
        handed = along(relay_w, [(0, 1), (3, 2)])
        outer = along(far_w, [(0, 2), (3, 1)])
        from_left = along(right_w, [(0, 1), (1, 2), (2, 3)])
        from_right = along(left_w, [(1, 0), (2, 1), (3, 2)])
        inner = along((far_w.astype(F32) + handed.astype(F32)).astype(BF16), [(1, 3), (2, 0)])
        messages = [own_w, from_left, from_right, outer, inner]
        down_sum, up_sum, gain_sum = total_call(messages, 1.0 / devices, half)
    else:
        (whole,) = weight_call(meta, saved, pairs, sums, ((7, 19),), parts, half, rank)
        down_sum, up_sum, gain_sum = total_call([whole], 1.0 / devices, half)
        scatter = functools.partial(lax.psum_scatter, axis_name="dp", scatter_dimension=1, tiled=True)
        down_sum, up_sum, gain_sum = scatter(down_sum), scatter(up_sum), scatter(gain_sum)
    return grads_out[None], down_sum[None], up_sum[None], gain_sum[None]


def solution(mesh):
    in_specs = (
        P(("groups", "dp"), None),
        P("groups"),
        P("groups"),
        P("section", None, "dp", None),
        P("section", None, "dp", None),
        P("section", None, None),
        P("dp", None),
        P(),
        P(),
    )
    out_specs = (
        P("section", ("groups", "dp"), None),
        P(("groups", "section"), None, "dp", None),
        P(("groups", "section"), None, "dp", None),
        P(("groups", "section"), None, "dp"),
    )
    return jax.shard_map(device_program, mesh=mesh, in_specs=in_specs, out_specs=out_specs, check_vma=False)
```
